512 devices in a mesh: tiles: 128 (over y, z, core), samp: 4 (over x).
Axes of the slice: x: 4, y: 4, z: 16, core: 2. Of those that a mesh axis runs over, the one named last changes fastest.
Arguments:
- samples: bfloat16 [256, 131072], P('samp', 'tiles'), may hold values from -6 to 6
- omega: float32 [1280, 512, 512], P('tiles', 'samp'), may hold values from -1 to 2, as said below
- coords: int32 [1280, 2], P('tiles'), may hold values from 0 to 255, as said below
Outputs:
- updated: float32 [1280, 512, 512], P('tiles', 'samp')
The draws below stay inside these ranges and needn't reach their ends.
Inputs may be any that keep to these rules, and one draw needn't show every extreme that they name: `coords`: tile k lies with index k // 10 of tiles. Write d for that index, and blocks d * 2 to (d + 1) * 2 - 1 as its own blocks; indices of devices wrap around. The first 2 tiles of d are the diagonal tiles (I, I) of its own blocks in order. Each other tile of d is (I, J) with I an own block and J a block of d + 1, or I a block of d - 1 and J a block of d + 1, or I < J both own blocks. No unordered pair of blocks appears twice in the whole list. `omega`: tiles with I == J are symmetric with diagonal entries from 0.5 to 2.
All inputs are finite; a program needn't handle non-finite values.
Results may differ from the reference program's by a relative error of at most 0.0023.
Values may be sent and summed in bfloat16 or wider, within the bound.
No kernel may reach another device: no remote copies, remote signals or barrier semaphores. Data moves between devices by JAX's collectives and lax.ppermute only.
A program may use at most 64 MiB of HBM per device.

```python
import jax
import jax.numpy as jnp
from jax import lax

B = 512
BLK_DEV = 2
TILE_DEV = 10
ITERS = 2
NB = 256
P_SIZE = 131072
NS = 256
TILES = 1280


def draw_coords(key, part):
    devices = NB // BLK_DEV

    def one_device(device, subkey):
        left_dev = (device - 1 + devices) % devices
        right_dev = (device + 1) % devices
        firsts = []
        seconds = []
        for first_pos in range(BLK_DEV):
            for second_pos in range(BLK_DEV):
                firsts.append(device * BLK_DEV + first_pos)
                seconds.append(right_dev * BLK_DEV + second_pos)
                firsts.append(left_dev * BLK_DEV + first_pos)
                seconds.append(right_dev * BLK_DEV + second_pos)
                if first_pos < second_pos:
                    firsts.append(device * BLK_DEV + first_pos)
                    seconds.append(device * BLK_DEV + second_pos)
        candidates = jnp.stack([jnp.stack(firsts), jnp.stack(seconds)], 1).astype(jnp.int32)
        order = jax.random.permutation(subkey, len(firsts))[:TILE_DEV - BLK_DEV]
        chosen = candidates[order]
        own_blocks = device * BLK_DEV + jnp.arange(BLK_DEV, dtype=jnp.int32)
        diagonal = jnp.stack([own_blocks, own_blocks], 1)
        return jnp.concatenate([diagonal, chosen], 0)
    subkeys = jax.random.split(jax.random.fold_in(key, 11), devices)
    result = jax.vmap(one_device)(jnp.arange(devices, dtype=jnp.int32), subkeys)
    return result.reshape(TILES, 2).astype(jnp.int32)


def draw_omega(key, part):
    key_off, key_diag = jax.random.split(jax.random.fold_in(key, 23), 2)
    raw = 0.03 * jax.random.normal(key_off, (TILES, B, B), jnp.float32)
    symmetric = (raw + jnp.swapaxes(raw, 1, 2)) * 0.7071
    slots = jnp.arange(TILES) % TILE_DEV
    is_diag = (slots < BLK_DEV)[:, None, None]
    tiles = jnp.where(is_diag, symmetric, raw)
    diag_vals = jnp.exp(jax.random.uniform(key_diag, (TILES, B), jnp.float32, jnp.log(0.5), jnp.log(2.0)))
    on_diagonal = jnp.eye(B, dtype=bool)[None]
    tiles = jnp.where(is_diag & on_diagonal, diag_vals[:, :, None], tiles)
    return tiles.astype(jnp.float32)


def levels(rng, extent, pieces, low, largest):
    def one(axis_at, blocks):
        steps = jax.random.uniform(jax.random.fold_in(jax.random.fold_in(rng, 6), axis_at), (blocks,), jnp.float32, low / len(pieces), largest / len(pieces))
        return jnp.repeat(jnp.exp(steps), extent[axis_at] // blocks).reshape((-1,) + (1,) * (len(extent) - axis_at - 1))

    gain = one(*pieces[0])
    for cut in pieces[1:]:
        gain = gain * one(*cut)
    return gain


def gaussian(own_key, dims, width, limit, pieces=(), held_as=jnp.bfloat16):
    values = width * jax.random.normal(own_key, dims, jnp.float32)
    if pieces:
        values = values * levels(own_key, dims, pieces, -0.22, 0.18)
    return jnp.clip(values, -limit, limit).astype(held_as)


def setup_inputs(seed: int = 0) -> dict:
    seeds = jax.random.split(jax.random.key(seed), 4)
    return {
        "samples": gaussian(seeds[0], (NS, P_SIZE), 1.0, 6.0, ((0, 4), (1, 128))),
        "omega": draw_omega(jax.random.fold_in(seeds[3], 71), 0),
        "coords": draw_coords(jax.random.fold_in(seeds[3], 71), 0),
    }


step_size = 0.25
penalty = 0.2

def take(matrix, start, count):
    return lax.dynamic_slice_in_dim(matrix, start, count, 1)

def put_add(totals, block, start):
    current = lax.dynamic_slice_in_dim(totals, start, block.shape[1], 1)
    return lax.dynamic_update_slice_in_dim(totals, current + block, start, 1)

def reference(samples, omega, coords):
    sample_full = samples.astype(jnp.float32)
    count = sample_full.shape[0]
    on_diagonal = jnp.eye(B, dtype=bool)
    for iteration in range(ITERS):
        omega_low = lax.optimization_barrier(omega.astype(jnp.bfloat16)).astype(jnp.float32)

        def contribute(totals, item):
            tile, pair = item
            row_start = pair[0] * B
            col_start = pair[1] * B
            off_diagonal = (pair[0] != pair[1]).astype(jnp.float32)
            to_col = jnp.dot(take(sample_full, row_start, B), tile, preferred_element_type=jnp.float32)
            to_row = jnp.dot(take(sample_full, col_start, B), tile.T, preferred_element_type=jnp.float32)
            totals = put_add(totals, to_col, col_start)
            totals = put_add(totals, to_row * off_diagonal, row_start)
            return (totals, None)
        products, unused = lax.scan(contribute, jnp.zeros(sample_full.shape, jnp.float32), (omega_low, coords))
        product_low = lax.optimization_barrier(products.astype(jnp.bfloat16)).astype(jnp.float32)

        def update(item):
            tile, pair = item
            row_start = pair[0] * B
            col_start = pair[1] * B
            first = jnp.dot(take(product_low, row_start, B).T, take(sample_full, col_start, B), preferred_element_type=jnp.float32)
            second = jnp.dot(take(sample_full, row_start, B).T, take(product_low, col_start, B), preferred_element_type=jnp.float32)
            grad = (first + second) / (2.0 * count)
            value = tile - step_size * grad
            shrunk = jnp.sign(value) * jnp.maximum(jnp.abs(value) - step_size * penalty, 0.0)
            positive = 0.5 * (value + jnp.sqrt(value * value + 4.0 * step_size))
            return jnp.where(on_diagonal & (pair[0] == pair[1]), positive, shrunk)
        omega = lax.map(update, (omega, coords))
    return omega
```

```python
import functools

import jax
import jax.numpy as jnp
from jax import lax
from jax.experimental import pallas as pl
from jax.experimental.pallas import tpu as pltpu
from jax.sharding import PartitionSpec as P

BLK_DEV = 2
step_size = 0.25
penalty = 0.2

VMEM = pl.BlockSpec(memory_space=pltpu.VMEM)
SMEM = pl.BlockSpec(memory_space=pltpu.SMEM)


def dot_nn(a, b):
    return jnp.dot(a, b, preferred_element_type=jnp.float32)


def dot_nt(a, b):
    return lax.dot_general(a, b, (((1,), (1,)), ((), ())), preferred_element_type=jnp.float32)


def shrink(value):
    level = step_size * penalty
    return value - jnp.clip(value, -level, level)


def position(coords, slot, side, first, blocks):
    at = coords[slot, side] - first
    at = jnp.where(at < 0, at + blocks, at)
    return jnp.where(at >= blocks, at - blocks, at)


def transpose_kernel(x_ref, o_ref):
    o_ref[...] = x_ref[...].T


def fill_samples(st, before, own, after):
    width = st.shape[1]
    for side, ref in enumerate((before, own, after)):
        for blk in range(BLK_DEV):
            st[side * BLK_DEV + blk] = ref[pl.ds(blk * width, width), :]


def fill_products(pt, before, own, after):
    rows = own.shape[1] // BLK_DEV
    for side, ref in enumerate((before, own, after)):
        for blk in range(BLK_DEV):
            for part in range(own.shape[0]):
                pt[side * BLK_DEV + blk, pl.ds(part * rows, rows), :] = ref[part, pl.ds(blk * rows, rows), :]


def put_totals(acc, down_ref, own_ref, up_ref):
    rows = acc.shape[1]
    for blk in range(BLK_DEV):
        at = pl.ds(blk * rows, rows)
        down_ref[at, :] = acc[blk].astype(jnp.bfloat16)
        own_ref[at, :] = acc[BLK_DEV + blk]
        up_ref[at, :] = acc[2 * BLK_DEV + blk].astype(jnp.bfloat16)


def first_kernel(blocks, coords, omega, parts, before, own, after, down_ref, own_ref, up_ref, ct_ref, st, acc):
    first = (lax.axis_index("tiles") - 1) * BLK_DEV
    tiles, rows, width = omega.shape
    fill_samples(st, before, own, after)
    acc[...] = jnp.zeros_like(acc)
    for slot in range(BLK_DEV):
        at = BLK_DEV + slot
        acc[at] = dot_nn(omega[slot].astype(jnp.bfloat16), st[at])

    def step(slot, carry):
        row = position(coords, slot, 0, first, blocks)
        col = position(coords, slot, 1, first, blocks)
        side = slot - BLK_DEV
        for part in range(width // rows):
            ct_ref[side, :, pl.ds(part * rows, rows)] = parts[part, side].T
        acc[row] += dot_nn(omega[slot].astype(jnp.bfloat16), st[col])
        acc[col] += dot_nn(ct_ref[side], st[row])
        return carry

    lax.fori_loop(BLK_DEV, tiles, step, 0)
    put_totals(acc, down_ref, own_ref, up_ref)


def gradient(pt, st, row, col, here):
    return dot_nt(pt[row, here, :], st[col]) + dot_nt(st[row, here, :], pt[col])


def diagonal(value, quarter):
    rows, width = value.shape
    row_ids = quarter * rows + lax.broadcasted_iota(jnp.int32, (rows, width), 0)
    col_ids = lax.broadcasted_iota(jnp.int32, (rows, width), 1)
    positive = 0.5 * (value + jnp.sqrt(value * value + 4.0 * step_size))
    return jnp.where(row_ids == col_ids, positive, shrink(value))


def middle_kernel(
    blocks, coords, omega, ct_ref, before, own, after, p_before, p_own, p_after,
    new_ref, down_ref, own_ref, up_ref, st, pt, acc,
):
    first = (lax.axis_index("tiles") - 1) * BLK_DEV
    quarter = lax.axis_index("samp")
    tiles, rows, width = omega.shape
    scale = step_size / (2.0 * st.shape[2])
    here = pl.ds(pl.multiple_of(quarter * rows, rows), rows)
    fill_samples(st, before, own, after)
    fill_products(pt, p_before, p_own, p_after)
    acc[...] = jnp.zeros_like(acc)
    for slot in range(BLK_DEV):
        at = BLK_DEV + slot
        tile = diagonal(omega[slot] - scale * gradient(pt, st, at, at, here), quarter)
        new_ref[slot] = tile
        acc[at] = dot_nn(tile.astype(jnp.bfloat16), st[at])

    def step(slot, carry):
        row = position(coords, slot, 0, first, blocks)
        col = position(coords, slot, 1, first, blocks)
        tile = shrink(omega[slot] - scale * gradient(pt, st, row, col, here))
        new_ref[slot] = tile
        acc[row] += dot_nn(tile.astype(jnp.bfloat16), st[col])
        held = ct_ref[slot - BLK_DEV].astype(jnp.float32)
        turned = shrink(held - scale * gradient(pt, st, col, row, here))
        acc[col] += dot_nn(turned.astype(jnp.bfloat16), st[row])
        return carry

    lax.fori_loop(BLK_DEV, tiles, step, 0)
    put_totals(acc, down_ref, own_ref, up_ref)


def last_kernel(blocks, coords, omega, before, own, after, p_before, p_own, p_after, new_ref, st, pt):
    first = (lax.axis_index("tiles") - 1) * BLK_DEV
    quarter = lax.axis_index("samp")
    tiles, rows, width = omega.shape
    scale = step_size / (2.0 * st.shape[2])
    here = pl.ds(pl.multiple_of(quarter * rows, rows), rows)
    fill_samples(st, before, own, after)
    fill_products(pt, p_before, p_own, p_after)
    for slot in range(BLK_DEV):
        at = BLK_DEV + slot
        new_ref[slot] = diagonal(omega[slot] - scale * gradient(pt, st, at, at, here), quarter)

    def step(slot, carry):
        row = position(coords, slot, 0, first, blocks)
        col = position(coords, slot, 1, first, blocks)
        new_ref[slot] = shrink(omega[slot] - scale * gradient(pt, st, row, col, here))
        return carry

    lax.fori_loop(BLK_DEV, tiles, step, 0)


def shards(samples, omega, coords):
    size = lax.axis_size("tiles")
    parts = lax.axis_size("samp")
    blocks = BLK_DEV * size
    tiles, rows, width = omega.shape
    others = tiles - BLK_DEV
    count = samples.shape[0] * parts
    own_width = samples.shape[1]
    up = [(i, (i + 1) % size) for i in range(size)]
    down = [(j, i) for i, j in up]
    bf16, f32 = jnp.bfloat16, jnp.float32

    def around(x):
        return lax.ppermute(x, "tiles", up), lax.ppermute(x, "tiles", down)

    gathered = lax.all_gather(samples, "samp", axis=0, tiled=True)
    st_own = pl.pallas_call(
        transpose_kernel, out_shape=jax.ShapeDtypeStruct((own_width, count), bf16),
        in_specs=[VMEM], out_specs=VMEM,
    )(gathered)
    st_before, st_after = around(st_own)
    pieces = omega[BLK_DEV:].astype(bf16).reshape(others, rows, parts, rows).transpose(2, 0, 1, 3)
    turned = lax.all_to_all(pieces, "samp", 0, 0)
    part_rows = BLK_DEV * rows
    half = jax.ShapeDtypeStruct((part_rows, count), bf16)
    whole = jax.ShapeDtypeStruct((part_rows, count), f32)
    st_scratch = pltpu.VMEM((3 * BLK_DEV, width, count), bf16)
    acc_scratch = pltpu.VMEM((3 * BLK_DEV, rows, count), f32)
    params = pltpu.CompilerParams(vmem_limit_bytes=48 << 20)
    down_part, own_part, up_part, ct = pl.pallas_call(
        functools.partial(first_kernel, blocks),
        out_shape=(half, whole, half, jax.ShapeDtypeStruct((others, rows, width), bf16)),
        in_specs=[SMEM] + [VMEM] * 5, out_specs=(VMEM,) * 4,
        scratch_shapes=[st_scratch, acc_scratch], compiler_params=params,
    )(coords, omega, turned, st_before, st_own, st_after)

    def products(down_part, own_part, up_part):
        from_before = lax.ppermute(up_part, "tiles", up)
        from_after = lax.ppermute(down_part, "tiles", down)
        total = own_part + from_before.astype(f32) + from_after.astype(f32)
        p_own = lax.all_gather(total.astype(bf16), "samp", axis=0, tiled=False)
        p_before, p_after = around(p_own)
        return p_before, p_own, p_after

    p = products(down_part, own_part, up_part)
    tile_shape = jax.ShapeDtypeStruct(omega.shape, f32)
    omega, down_part, own_part, up_part = pl.pallas_call(
        functools.partial(middle_kernel, blocks),
        out_shape=(tile_shape, half, whole, half),
        in_specs=[SMEM] + [VMEM] * 8, out_specs=(VMEM,) * 4,
        scratch_shapes=[st_scratch, st_scratch, acc_scratch], compiler_params=params,
    )(coords, omega, ct, st_before, st_own, st_after, *p)
    p = products(down_part, own_part, up_part)
    return pl.pallas_call(
        functools.partial(last_kernel, blocks),
        out_shape=tile_shape,
        in_specs=[SMEM] + [VMEM] * 7, out_specs=VMEM,
        scratch_shapes=[st_scratch, st_scratch], compiler_params=params,
    )(coords, omega, st_before, st_own, st_after, *p)


def solution(mesh):
    in_specs = (P("samp", "tiles"), P("tiles", "samp", None), P("tiles", None))
    out_specs = P("tiles", "samp", None)
    return jax.shard_map(shards, mesh=mesh, in_specs=in_specs, out_specs=out_specs, check_vma=False)
```

```python
import functools

import jax
import jax.numpy as jnp
from jax import lax
from jax.experimental import pallas as pl
from jax.experimental.pallas import tpu as pltpu
from jax.sharding import PartitionSpec as P


BLK_DEV = 2
step_size = 0.25
penalty = 0.2

VMEM = pl.BlockSpec(memory_space=pltpu.VMEM)
SMEM = pl.BlockSpec(memory_space=pltpu.SMEM)
ANY = pl.BlockSpec(memory_space=pl.ANY)
bf16, f32 = jnp.bfloat16, jnp.float32

OWN_PAIR = 8
LIMIT = 12 << 20


def dot_nn(a, b):
    return jnp.dot(a, b, preferred_element_type=f32)


def dot_nt(a, b):
    return lax.dot_general(a, b, (((1,), (1,)), ((), ())), preferred_element_type=f32)


def shrink(value):
    level = step_size * penalty
    return value - jnp.clip(value, -level, level)


def shrink_diagonal(value, quarter):
    rows, width = value.shape
    row_ids = quarter * rows + lax.broadcasted_iota(jnp.int32, (rows, width), 0)
    col_ids = lax.broadcasted_iota(jnp.int32, (rows, width), 1)
    positive = 0.5 * (value + jnp.sqrt(value * value + 4.0 * step_size))
    return jnp.where(row_ids == col_ids, positive, shrink(value))


def find_slots(blocks, coords, slot_of):
    first = (lax.axis_index("tiles") - 1) * BLK_DEV
    for pair in range(OWN_PAIR + 1):
        slot_of[pair] = 0

    def place(slot, side):
        at = coords[slot, side] - first
        at = jnp.where(at < 0, at + blocks, at)
        return jnp.where(at >= blocks, at - blocks, at)

    for slot in range(BLK_DEV, coords.shape[0]):
        row, col = place(slot, 0), place(slot, 1)
        pair = jnp.where(col >= 2 * BLK_DEV, (col - 2 * BLK_DEV) * 2 * BLK_DEV + row, OWN_PAIR)
        slot_of[pair] = slot


def is_even():
    return lax.rem(lax.axis_index("tiles"), 2) == 0


def cut_kernel(omega, gathered, out, held, sems):
    rows = omega.shape[1]
    copies = []
    for part in range(out.shape[0]):
        for slot in range(BLK_DEV, omega.shape[0]):
            held[part, slot - BLK_DEV] = omega[slot, :, part * rows : (part + 1) * rows].astype(bf16)
        copies.append(pltpu.make_async_copy(held.at[part], out.at[part], sems.at[part]))
        copies[-1].start()
    for copy in copies:
        copy.wait()


def rows_kernel(
    blocks, coords, omega, s_own, s_cross, s_chip,
    s_before, s_after, stq, t_before, t_own, slot_of, mats,
):
    rows, width = omega.shape[1:]
    quarter = lax.axis_index("samp")
    find_slots(blocks, coords, slot_of)

    @pl.when(is_even())
    def _():
        s_before[...] = s_cross[...]
        s_after[...] = s_chip[...]

    @pl.when(jnp.logical_not(is_even()))
    def _():
        s_before[...] = s_chip[...]
        s_after[...] = s_cross[...]

    for side, ref in enumerate((s_before, s_own, s_after)):
        for blk in range(BLK_DEV):
            at = pl.multiple_of(blk * width + quarter * rows, rows)
            stq[side, blk * rows : (blk + 1) * rows, :] = ref[:, pl.ds(at, rows)].T

    def convert(pair, carry):
        slot = slot_of[pair]

        @pl.when(slot > 0)
        def _():
            mats[pair] = omega[slot].astype(bf16)

        @pl.when(slot == 0)
        def _():
            mats[pair] = jnp.zeros_like(mats[pair])

        return carry

    lax.fori_loop(0, OWN_PAIR + 1, convert, 0)
    total = dot_nt(mats[0:4].reshape(4 * rows, width), s_after[:, :width])
    total += dot_nt(mats[4:8].reshape(4 * rows, width), s_after[:, width:])
    t_before[...] = total[: 2 * rows].astype(bf16)
    left, right = s_own[:, :width], s_own[:, width:]
    t_own[:rows] = total[2 * rows : 3 * rows] + (
        dot_nt(omega[0].astype(bf16), left) + dot_nt(mats[OWN_PAIR], right)
    )
    t_own[rows:] = total[3 * rows :] + dot_nt(omega[1].astype(bf16), right)


def send_halves(cross, chip, before, after):
    @pl.when(is_even())
    def _():
        cross[...] = before
        chip[...] = after

    @pl.when(jnp.logical_not(is_even()))
    def _():
        cross[...] = after
        chip[...] = before


def cols_kernel(
    blocks, coords, parts, s_before, s_own, s_after, t_before, t_own,
    turned, cross, chip, own, slot_of,
):
    count, rows = parts.shape[0], parts.shape[2]
    width = count * rows
    find_slots(blocks, coords, slot_of)

    def convert(pair, carry):
        slot = slot_of[pair]
        unit = jnp.where(pair == OWN_PAIR, OWN_PAIR, lax.rem(pair, 4) * 2 + pair // 4)

        @pl.when(slot > 0)
        def _():
            for part in range(count):
                turned[unit, :, part * rows : (part + 1) * rows] = parts[part, slot - BLK_DEV].T

        @pl.when(slot == 0)
        def _():
            turned[unit] = jnp.zeros_like(turned[unit])

        return carry

    lax.fori_loop(0, OWN_PAIR + 1, convert, 0)
    total = jnp.zeros(own.shape, f32)
    for a in range(2 * BLK_DEV):
        source = (s_before, s_own)[a // BLK_DEV]
        blk = a % BLK_DEV
        total += dot_nt(turned[2 * a : 2 * a + 2].reshape(2 * rows, width), source[:, blk * width : (blk + 1) * width])
    send_halves(cross, chip, t_before[...], total.astype(bf16))
    own[:rows] = t_own[:rows]
    own[rows:] = t_own[rows:] + dot_nt(turned[OWN_PAIR], s_own[:, :width])


def natural(out, pieces):
    count, both = pieces.shape[0], pieces.shape[1]
    rows = both // BLK_DEV
    for blk in range(BLK_DEV):
        for part in range(count):
            at = (blk * count + part) * rows
            out[at : at + rows, :] = pieces[part, blk * rows : (blk + 1) * rows, :]


def own_kernel(blocks, last, *refs):
    if last:
        coords, held, s_own, stq, p_own, out, slot_of, grad, nat_own, tiles, sems = refs
    else:
        coords, omega, turned, s_own, stq, p_own, tiles, t_own, nat_own, slot_of, grad, mats = refs
    rows, width = grad.shape[0] // 2, grad.shape[1] // 2
    quarter = lax.axis_index("samp")
    scale = step_size / (2.0 * s_own.shape[0])
    find_slots(blocks, coords, slot_of)
    natural(nat_own, p_own)
    grad[...] = dot_nn(p_own[quarter], s_own[...]) + dot_nt(stq[1], nat_own[...])
    slot = slot_of[OWN_PAIR]
    for i in range(BLK_DEV):
        old = held[i] if last else omega[i]
        here = grad[i * rows : (i + 1) * rows, i * width : (i + 1) * width]
        tiles[i] = shrink_diagonal(old - scale * here, quarter)
    old = held[2] if last else omega[slot]
    tiles[2] = shrink(old - scale * grad[:rows, width:])
    if last:
        copies = [pltpu.make_async_copy(tiles.at[i], out.at[i], sems.at[i]) for i in range(BLK_DEV)]
        for copy in copies:
            copy.start()

        @pl.when(slot > 0)
        def _():
            copy = pltpu.make_async_copy(tiles.at[2], out.at[slot], sems.at[2])
            copy.start()
            copy.wait()

        for copy in copies:
            copy.wait()
        return
    mats[:rows, :width] = tiles[0].astype(bf16)
    mats[rows:, width:] = tiles[1].astype(bf16)

    @pl.when(slot > 0)
    def _():
        mats[:rows, width:] = tiles[2].astype(bf16)
        there = turned[OWN_PAIR].astype(f32) - scale * grad[rows:, :width]
        mats[rows:, :width] = shrink(there).astype(bf16)

    @pl.when(slot == 0)
    def _():
        mats[:rows, width:] = jnp.zeros((rows, width), bf16)
        mats[rows:, :width] = jnp.zeros((rows, width), bf16)

    t_own[...] = dot_nt(mats[...], s_own[...])


def order_halo(nat, ptq, p_cross, p_chip, quarter):
    even = is_even()
    for ref, at in ((p_cross, jnp.where(even, 0, 1)), (p_chip, jnp.where(even, 1, 0))):
        natural(nat.at[at], ref)
        ptq[at] = ref[quarter]


def update_rows(slot_of, source, grad, a_base, scale, tiles, mats):
    rows, width = grad.shape[0] // 2, grad.shape[1] // 2
    for a in range(2):
        for b in range(2):
            slot = slot_of[b * 4 + a_base + a]
            here = grad[a * rows : (a + 1) * rows, b * width : (b + 1) * width]
            tile = shrink(source[slot] - scale * here)
            tiles[a * 2 + b] = tile
            spot = (slice(a * rows, (a + 1) * rows), slice(b * width, (b + 1) * width))
            mats[spot] = jnp.where(slot > 0, tile, 0.0).astype(bf16)


def outer_kernel(
    blocks, coords, omega, turned, s_before, s_own, s_after, stq, nat_own, p_cross, p_chip,
    tiles, cross, chip, slot_of, nat, ptq, grad, mats, half,
):
    rows, width = omega.shape[1:]
    quarter = lax.axis_index("samp")
    scale = step_size / (2.0 * s_own.shape[0])
    find_slots(blocks, coords, slot_of)
    order_halo(nat, ptq, p_cross, p_chip, quarter)
    total = jnp.zeros(cross.shape, f32)
    for a in range(2 * BLK_DEV):
        blk = a % BLK_DEV
        at = slice(blk * width, (blk + 1) * width)
        source = (s_before, s_own)[a // BLK_DEV][:, at]
        product = (nat.at[0], nat_own)[a // BLK_DEV][at, :]
        half[...] = dot_nn(ptq[1], source) + dot_nt(stq[2], product)
        for b in range(BLK_DEV):
            tile = shrink(turned[2 * a + b].astype(f32) - scale * half[b * rows : (b + 1) * rows, :])
            tile = jnp.where(slot_of[b * 4 + a] > 0, tile, 0.0)
            mats[b * rows : (b + 1) * rows, at] = tile.astype(bf16)
        total += dot_nt(mats[:, at], source)
    after = total.astype(bf16)
    grad[...] = dot_nn(ptq[0], s_after[...]) + dot_nt(stq[0], nat[1])
    update_rows(slot_of, omega, grad, 0, scale, tiles, mats)
    before = dot_nt(mats[...], s_after[...]).astype(bf16)
    send_halves(cross, chip, before, after)


def inner_kernel(
    blocks, coords, omega, s_own, s_after, stq, p_own, p_cross, p_chip, t_own,
    tiles, own, slot_of, nat, ptq, grad, mats,
):
    quarter = lax.axis_index("samp")
    scale = step_size / (2.0 * s_own.shape[0])
    find_slots(blocks, coords, slot_of)
    order_halo(nat, ptq, p_cross, p_chip, quarter)
    grad[...] = dot_nn(p_own[quarter], s_after[...]) + dot_nt(stq[1], nat[1])
    update_rows(slot_of, omega, grad, BLK_DEV, scale, tiles, mats)
    own[...] = t_own[...] + dot_nt(mats[...], s_after[...])


def last_kernel(
    blocks, coords, outer, inner, s_after, stq, p_own, p_cross, p_chip, begun,
    out, slot_of, nat, ptq, grad, tiles, sems,
):
    rows, width = tiles.shape[1:]
    quarter = lax.axis_index("samp")
    scale = step_size / (2.0 * s_after.shape[0])
    find_slots(blocks, coords, slot_of)
    order_halo(nat, ptq, p_cross, p_chip, quarter)
    for group in range(2):
        lhs = ptq[0] if group == 0 else p_own[quarter]
        grad[group] = dot_nn(lhs, s_after[...]) + dot_nt(stq[group], nat[1])
        for a in range(2):
            for b in range(2):
                unit = group * 4 + a * 2 + b
                slot = slot_of[b * 4 + group * 2 + a]
                here = grad[group, a * rows : (a + 1) * rows, b * width : (b + 1) * width]
                tiles[unit] = shrink((outer, inner)[group][a * 2 + b] - scale * here)

                @pl.when(slot > 0)
                def _(unit=unit, slot=slot):
                    pltpu.make_async_copy(tiles.at[unit], out.at[slot], sems.at[unit]).start()

    for group in range(2):
        for a in range(2):
            for b in range(2):
                unit = group * 4 + a * 2 + b
                slot = slot_of[b * 4 + group * 2 + a]

                @pl.when(slot > 0)
                def _(unit=unit, slot=slot):
                    pltpu.make_async_copy(tiles.at[unit], out.at[slot], sems.at[unit]).wait()


def shards(samples, omega, coords):
    size = lax.axis_size("tiles")
    parts = lax.axis_size("samp")
    blocks = BLK_DEV * size
    tiles, rows, width = omega.shape
    others = tiles - BLK_DEV
    count = samples.shape[0] * parts
    wide = samples.shape[1]
    both = BLK_DEV * rows
    chip = [(i, i ^ 1) for i in range(size)]
    cross = [(i, (i - 1) % size if i % 2 == 0 else (i + 1) % size) for i in range(size)]
    shape = jax.ShapeDtypeStruct
    slots = pltpu.SMEM((OWN_PAIR + 1,), jnp.int32)
    params = pltpu.CompilerParams(vmem_limit_bytes=LIMIT)

    def call(body, in_specs, outs, scratch, macs, moved, aliases=None, out_specs=None):
        several = isinstance(outs, tuple)
        specs = out_specs or ((VMEM,) * len(outs) if several else VMEM)
        return pl.pallas_call(
            body, out_shape=outs, in_specs=in_specs, out_specs=specs, scratch_shapes=scratch,
            compiler_params=params, input_output_aliases=aliases or {},
            cost_estimate=pl.CostEstimate(flops=2 * macs, bytes_accessed=moved, transcendentals=0),
        )

    def exchange(to_cross, to_chip):
        from_chip = lax.ppermute(to_chip, "tiles", chip)
        from_cross = lax.ppermute(to_cross, "tiles", cross)
        return from_cross, from_chip

    s_own = lax.all_gather(samples, "samp", axis=0, tiled=True)
    pieces = call(
        cut_kernel, [VMEM, ANY], shape((parts, others, rows, rows), bf16),
        [pltpu.VMEM((parts, others, rows, rows), bf16), pltpu.SemaphoreType.DMA((parts,))], 0, 4 << 20, out_specs=ANY,
    )(omega, s_own)
    turned_parts = lax.all_to_all(pieces, "samp", 0, 0)
    s_cross, s_chip = exchange(s_own, s_own)

    window = shape((count, wide), bf16)
    part = shape((both, count), bf16)
    full = shape((both, count), f32)
    held = pltpu.VMEM((OWN_PAIR + 1, rows, width), bf16)
    unit = rows * width * count
    s_before, s_after, stq, t_before, t_own = call(
        functools.partial(rows_kernel, blocks), [SMEM] + [VMEM] * 4,
        (window, window, shape((3, both, count), bf16), part, full), [slots, held], 11 * unit, 4 << 20,
    )(coords, omega, s_own, s_cross, s_chip)
    turned, to_cross, to_chip, own = call(
        functools.partial(cols_kernel, blocks), [SMEM] + [VMEM] * 6,
        (shape((OWN_PAIR + 1, rows, width), bf16), part, part, full), [slots], 9 * unit, 3 << 20,
    )(coords, turned_parts, s_before, s_own, s_after, t_before, t_own)

    def products(to_cross, to_chip, finish):
        from_cross, from_chip = exchange(to_cross, to_chip)
        tiles, own = finish()
        total = own + from_cross.astype(f32) + from_chip.astype(f32)
        p_own = lax.all_gather(total.astype(bf16), "samp", axis=0, tiled=False)
        p_cross, p_chip = exchange(p_own, p_own)
        return tiles, p_own, p_cross, p_chip

    grad = pltpu.VMEM((both, wide), f32)
    mats = pltpu.VMEM((both, wide), bf16)
    nat = pltpu.VMEM((2, wide, count), bf16)
    ptq = pltpu.VMEM((2, both, count), bf16)
    four = shape((4, rows, width), f32)

    _, p_own, p_cross, p_chip = products(to_cross, to_chip, lambda: (None, own))
    mine, t_own, nat_own = call(
        functools.partial(own_kernel, blocks, False), [SMEM] + [VMEM] * 5,
        (shape((3, rows, width), f32), full, shape((wide, count), bf16)), [slots, grad, mats], 12 * unit, 4 << 20,
    )(coords, omega, turned, s_own, stq, p_own)
    outer, to_cross, to_chip = call(
        functools.partial(outer_kernel, blocks), [SMEM] + [VMEM] * 9,
        (four, part, part), [slots, nat, ptq, grad, mats, pltpu.VMEM((both, width), f32)], 36 * unit, 6 << 20,
    )(coords, omega, turned, s_before, s_own, s_after, stq, nat_own, p_cross, p_chip)

    def finish():
        return call(
            functools.partial(inner_kernel, blocks), [SMEM] + [VMEM] * 8,
            (four, full), [slots, nat, ptq, grad, mats], 12 * unit, 4 << 20,
        )(coords, omega, s_own, s_after, stq, p_own, p_cross, p_chip, t_own)

    inner, p_own, p_cross, p_chip = products(to_cross, to_chip, finish)
    whole = shape(omega.shape, f32)
    begun = call(
        functools.partial(own_kernel, blocks, True), [SMEM] + [VMEM] * 4, whole,
        [slots, grad, pltpu.VMEM((wide, count), bf16), pltpu.VMEM((3, rows, width), f32), pltpu.SemaphoreType.DMA((3,))],
        8 * unit, 3 << 20, out_specs=ANY,
    )(coords, mine, s_own, stq, p_own)
    return call(
        functools.partial(last_kernel, blocks), [SMEM] + [VMEM] * 7 + [ANY], whole,
        [slots, nat, ptq, pltpu.VMEM((2, both, wide), f32), pltpu.VMEM((8, rows, width), f32), pltpu.SemaphoreType.DMA((8,))],
        16 * unit, 6 << 20, aliases={8: 0}, out_specs=ANY,
    )(coords, outer, inner, s_after, stq, p_own, p_cross, p_chip, begun)


def solution(mesh):
    in_specs = (P("samp", "tiles"), P("tiles", "samp", None), P("tiles", None))
    out_specs = P("tiles", "samp", None)

    return jax.shard_map(shards, mesh=mesh, in_specs=in_specs, out_specs=out_specs, check_vma=False)
```

```python
import functools

import jax
import jax.numpy as jnp
from jax import lax
from jax.experimental import pallas as pl
from jax.experimental.pallas import tpu as pltpu
from jax.sharding import PartitionSpec as P


BLK_DEV = 2
step_size = 0.25
penalty = 0.2

VMEM = pl.BlockSpec(memory_space=pltpu.VMEM)
SMEM = pl.BlockSpec(memory_space=pltpu.SMEM)
ANY = pl.BlockSpec(memory_space=pl.ANY)
bf16, f32 = jnp.bfloat16, jnp.float32

OWN_PAIR = 8
LIMIT = 12 << 20


def dot_nn(a, b):
    return jnp.dot(a, b, preferred_element_type=f32)


def dot_nt(a, b):
    return lax.dot_general(a, b, (((1,), (1,)), ((), ())), preferred_element_type=f32)


def shrink(value):
    level = step_size * penalty
    return value - jnp.clip(value, -level, level)


def shrink_diagonal(value, quarter):
    rows, width = value.shape
    row_ids = quarter * rows + lax.broadcasted_iota(jnp.int32, (rows, width), 0)
    col_ids = lax.broadcasted_iota(jnp.int32, (rows, width), 1)
    positive = 0.5 * (value + jnp.sqrt(value * value + 4.0 * step_size))
    return jnp.where(row_ids == col_ids, positive, shrink(value))


def find_slots(blocks, coords, slot_of):
    first = (lax.axis_index("tiles") - 1) * BLK_DEV
    for pair in range(OWN_PAIR + 1):
        slot_of[pair] = 0

    def place(slot, side):
        at = coords[slot, side] - first
        at = jnp.where(at < 0, at + blocks, at)
        return jnp.where(at >= blocks, at - blocks, at)

    for slot in range(BLK_DEV, coords.shape[0]):
        row, col = place(slot, 0), place(slot, 1)
        pair = jnp.where(col >= 2 * BLK_DEV, (col - 2 * BLK_DEV) * 2 * BLK_DEV + row, OWN_PAIR)
        slot_of[pair] = slot


def is_even():
    return lax.rem(lax.axis_index("tiles"), 2) == 0


def cut_kernel(omega, out, held, pieces, in_sems, out_sems):
    rows = omega.shape[1]
    others = held.shape[0]
    loads = [
        pltpu.make_async_copy(omega.at[BLK_DEV + k], held.at[k], in_sems.at[k]) for k in range(others)
    ]
    for load in loads:
        load.start()
    stores = []
    for k in range(others):
        loads[k].wait()
        for part in range(out.shape[0]):
            pieces[part, k] = held[k, :, part * rows : (part + 1) * rows].astype(bf16)
        stores.append(pltpu.make_async_copy(pieces.at[:, k], out.at[:, k], out_sems.at[k]))
        stores[-1].start()
    for store in stores:
        store.wait()


def send_halves(cross, chip, before, after):
    @pl.when(is_even())
    def _():
        cross[...] = before
        chip[...] = after

    @pl.when(jnp.logical_not(is_even()))
    def _():
        cross[...] = after
        chip[...] = before


def begin_kernel(
    blocks, coords, omega, parts, s_own, s_cross, s_chip,
    s_before, s_after, stq, turned, cross, chip, own, slot_of, mats,
):
    rows, width = omega.shape[1:]
    quarter = lax.axis_index("samp")
    find_slots(blocks, coords, slot_of)

    @pl.when(is_even())
    def _():
        s_before[...] = s_cross[...]
        s_after[...] = s_chip[...]

    @pl.when(jnp.logical_not(is_even()))
    def _():
        s_before[...] = s_chip[...]
        s_after[...] = s_cross[...]

    def convert(pair, carry):
        slot = slot_of[pair]
        unit = jnp.where(pair == OWN_PAIR, OWN_PAIR, lax.rem(pair, 4) * 2 + pair // 4)

        @pl.when(slot > 0)
        def _():
            mats[pair] = omega[slot].astype(bf16)
            for part in range(width // rows):
                turned[unit, :, part * rows : (part + 1) * rows] = parts[part, slot - BLK_DEV].T

        @pl.when(slot == 0)
        def _():
            mats[pair] = jnp.zeros_like(mats[pair])
            turned[unit] = jnp.zeros_like(turned[unit])

        return carry

    lax.fori_loop(0, OWN_PAIR + 1, convert, 0)
    total = dot_nt(mats[0:4].reshape(4 * rows, width), s_after[:, :width])
    total += dot_nt(mats[4:8].reshape(4 * rows, width), s_after[:, width:])
    left, right = s_own[:, :width], s_own[:, width:]
    own[:rows] = total[2 * rows : 3 * rows] + (
        dot_nt(omega[0].astype(bf16), left) + dot_nt(mats[OWN_PAIR], right)
    )
    own[rows:] = total[3 * rows :] + (
        dot_nt(omega[1].astype(bf16), right) + dot_nt(turned[OWN_PAIR], left)
    )
    after = jnp.zeros(own.shape, f32)
    for a in range(2 * BLK_DEV):
        source = (s_before, s_own)[a // BLK_DEV]
        blk = a % BLK_DEV
        after += dot_nt(turned[2 * a : 2 * a + 2].reshape(2 * rows, width), source[:, blk * width : (blk + 1) * width])
    send_halves(cross, chip, total[: 2 * rows].astype(bf16), after.astype(bf16))
    for side, ref in enumerate((s_before, s_own, s_after)):
        for blk in range(BLK_DEV):
            at = pl.multiple_of(blk * width + quarter * rows, rows)
            stq[side, blk * rows : (blk + 1) * rows, :] = ref[:, pl.ds(at, rows)].T


def natural(out, pieces):
    count, both = pieces.shape[0], pieces.shape[1]
    rows = both // BLK_DEV
    for blk in range(BLK_DEV):
        for part in range(count):
            at = (blk * count + part) * rows
            out[at : at + rows, :] = pieces[part, blk * rows : (blk + 1) * rows, :]


def own_kernel(blocks, last, *refs):
    if last:
        coords, held, s_own, stq, p_own, out, slot_of, grad, nat_own, tiles, sems = refs
    else:
        coords, omega, turned, s_own, stq, p_own, tiles, t_own, nat_own, slot_of, grad, mats = refs
    rows, width = grad.shape[0] // 2, grad.shape[1] // 2
    quarter = lax.axis_index("samp")
    scale = step_size / (2.0 * s_own.shape[0])
    find_slots(blocks, coords, slot_of)
    natural(nat_own, p_own)
    grad[...] = dot_nn(p_own[quarter], s_own[...]) + dot_nt(stq[1], nat_own[...])
    slot = slot_of[OWN_PAIR]
    for i in range(BLK_DEV):
        old = held[i] if last else omega[i]
        here = grad[i * rows : (i + 1) * rows, i * width : (i + 1) * width]
        tiles[i] = shrink_diagonal(old - scale * here, quarter)
    old = held[2] if last else omega[slot]
    tiles[2] = shrink(old - scale * grad[:rows, width:])
    if last:
        copies = [pltpu.make_async_copy(tiles.at[i], out.at[i], sems.at[i]) for i in range(BLK_DEV)]
        for copy in copies:
            copy.start()

        @pl.when(slot > 0)
        def _():
            copy = pltpu.make_async_copy(tiles.at[2], out.at[slot], sems.at[2])
            copy.start()
            copy.wait()

        for copy in copies:
            copy.wait()
        return
    mats[:rows, :width] = tiles[0].astype(bf16)
    mats[rows:, width:] = tiles[1].astype(bf16)

    @pl.when(slot > 0)
    def _():
        mats[:rows, width:] = tiles[2].astype(bf16)
        there = turned[OWN_PAIR].astype(f32) - scale * grad[rows:, :width]
        mats[rows:, :width] = shrink(there).astype(bf16)

    @pl.when(slot == 0)
    def _():
        mats[:rows, width:] = jnp.zeros((rows, width), bf16)
        mats[rows:, :width] = jnp.zeros((rows, width), bf16)

    t_own[...] = dot_nt(mats[...], s_own[...])


def order_halo(nat, ptq, p_cross, p_chip, quarter):
    even = is_even()
    for ref, at in ((p_cross, jnp.where(even, 0, 1)), (p_chip, jnp.where(even, 1, 0))):
        natural(nat.at[at], ref)
        ptq[at] = ref[quarter]


def update_rows(slot_of, source, grad, a_base, scale, tiles, mats):
    rows, width = grad.shape[0] // 2, grad.shape[1] // 2
    for a in range(2):
        for b in range(2):
            slot = slot_of[b * 4 + a_base + a]
            here = grad[a * rows : (a + 1) * rows, b * width : (b + 1) * width]
            tile = shrink(source[slot] - scale * here)
            tiles[a * 2 + b] = tile
            spot = (slice(a * rows, (a + 1) * rows), slice(b * width, (b + 1) * width))
            mats[spot] = jnp.where(slot > 0, tile, 0.0).astype(bf16)


def outer_kernel(
    blocks, coords, omega, turned, s_before, s_own, s_after, stq, nat_own, p_cross, p_chip,
    tiles, cross, chip, slot_of, nat, ptq, grad, mats, half,
):
    rows, width = omega.shape[1:]
    quarter = lax.axis_index("samp")
    scale = step_size / (2.0 * s_own.shape[0])
    find_slots(blocks, coords, slot_of)
    order_halo(nat, ptq, p_cross, p_chip, quarter)
    total = jnp.zeros(cross.shape, f32)
    for a in range(2 * BLK_DEV):
        blk = a % BLK_DEV
        at = slice(blk * width, (blk + 1) * width)
        source = (s_before, s_own)[a // BLK_DEV][:, at]
        product = (nat.at[0], nat_own)[a // BLK_DEV][at, :]
        half[...] = dot_nn(ptq[1], source) + dot_nt(stq[2], product)
        for b in range(BLK_DEV):
            tile = shrink(turned[2 * a + b].astype(f32) - scale * half[b * rows : (b + 1) * rows, :])
            tile = jnp.where(slot_of[b * 4 + a] > 0, tile, 0.0)
            mats[b * rows : (b + 1) * rows, at] = tile.astype(bf16)
        total += dot_nt(mats[:, at], source)
    after = total.astype(bf16)
    grad[...] = dot_nn(ptq[0], s_after[...]) + dot_nt(stq[0], nat[1])
    update_rows(slot_of, omega, grad, 0, scale, tiles, mats)
    before = dot_nt(mats[...], s_after[...]).astype(bf16)
    send_halves(cross, chip, before, after)


def inner_kernel(
    blocks, coords, omega, s_own, s_after, stq, p_own, p_cross, p_chip, t_own,
    tiles, own, slot_of, nat, ptq, grad, mats,
):
    quarter = lax.axis_index("samp")
    scale = step_size / (2.0 * s_own.shape[0])
    find_slots(blocks, coords, slot_of)
    order_halo(nat, ptq, p_cross, p_chip, quarter)
    grad[...] = dot_nn(p_own[quarter], s_after[...]) + dot_nt(stq[1], nat[1])
    update_rows(slot_of, omega, grad, BLK_DEV, scale, tiles, mats)
    own[...] = t_own[...] + dot_nt(mats[...], s_after[...])


def last_kernel(
    blocks, coords, outer, inner, s_after, stq, p_own, p_cross, p_chip, begun,
    out, slot_of, nat, ptq, grad, tiles, sems,
):
    rows, width = tiles.shape[1:]
    quarter = lax.axis_index("samp")
    scale = step_size / (2.0 * s_after.shape[0])
    find_slots(blocks, coords, slot_of)
    order_halo(nat, ptq, p_cross, p_chip, quarter)
    for group in range(2):
        lhs = ptq[0] if group == 0 else p_own[quarter]
        grad[group] = dot_nn(lhs, s_after[...]) + dot_nt(stq[group], nat[1])
        for a in range(2):
            for b in range(2):
                unit = group * 4 + a * 2 + b
                slot = slot_of[b * 4 + group * 2 + a]
                here = grad[group, a * rows : (a + 1) * rows, b * width : (b + 1) * width]
                tiles[unit] = shrink((outer, inner)[group][a * 2 + b] - scale * here)

                @pl.when(slot > 0)
                def _(unit=unit, slot=slot):
                    pltpu.make_async_copy(tiles.at[unit], out.at[slot], sems.at[unit]).start()

    for group in range(2):
        for a in range(2):
            for b in range(2):
                unit = group * 4 + a * 2 + b
                slot = slot_of[b * 4 + group * 2 + a]

                @pl.when(slot > 0)
                def _(unit=unit, slot=slot):
                    pltpu.make_async_copy(tiles.at[unit], out.at[slot], sems.at[unit]).wait()


def shards(samples, omega, coords):
    size = lax.axis_size("tiles")
    parts = lax.axis_size("samp")
    blocks = BLK_DEV * size
    tiles, rows, width = omega.shape
    others = tiles - BLK_DEV
    count = samples.shape[0] * parts
    wide = samples.shape[1]
    both = BLK_DEV * rows
    chip = [(i, i ^ 1) for i in range(size)]
    cross = [(i, (i - 1) % size if i % 2 == 0 else (i + 1) % size) for i in range(size)]
    shape = jax.ShapeDtypeStruct
    slots = pltpu.SMEM((OWN_PAIR + 1,), jnp.int32)
    params = pltpu.CompilerParams(vmem_limit_bytes=LIMIT)

    def call(body, in_specs, outs, scratch, macs, moved, aliases=None, out_specs=None):
        several = isinstance(outs, tuple)
        specs = out_specs or ((VMEM,) * len(outs) if several else VMEM)
        return pl.pallas_call(
            body, out_shape=outs, in_specs=in_specs, out_specs=specs, scratch_shapes=scratch,
            compiler_params=params, input_output_aliases=aliases or {},
            cost_estimate=pl.CostEstimate(flops=2 * macs, bytes_accessed=moved, transcendentals=0),
        )

    def exchange(to_cross, to_chip):
        from_chip = lax.ppermute(to_chip, "tiles", chip)
        from_cross = lax.ppermute(to_cross, "tiles", cross)
        return from_cross, from_chip

    def spread(x):
        return lax.all_to_all(jnp.broadcast_to(x[None], (parts,) + x.shape), "samp", 0, 0)

    s_own = spread(samples).reshape(count, wide)
    pieces = call(
        cut_kernel, [ANY], shape((parts, others, rows, rows), bf16),
        [
            pltpu.VMEM((others, rows, width), f32), pltpu.VMEM((parts, others, rows, rows), bf16),
            pltpu.SemaphoreType.DMA((others,)), pltpu.SemaphoreType.DMA((others,)),
        ],
        0, 4 << 20, out_specs=ANY,
    )(omega)
    turned_parts = lax.all_to_all(pieces, "samp", 0, 0)
    s_cross, s_chip = exchange(s_own, s_own)

    window = shape((count, wide), bf16)
    part = shape((both, count), bf16)
    full = shape((both, count), f32)
    unit = rows * width * count
    s_before, s_after, stq, turned, to_cross, to_chip, own = call(
        functools.partial(begin_kernel, blocks), [SMEM] + [VMEM] * 5,
        (window, window, shape((3, both, count), bf16), shape((OWN_PAIR + 1, rows, width), bf16), part, part, full),
        [slots, pltpu.VMEM((OWN_PAIR + 1, rows, width), bf16)], 20 * unit, 6 << 20,
    )(coords, omega, turned_parts, s_own, s_cross, s_chip)

    def products(to_cross, to_chip, finish):
        from_cross, from_chip = exchange(to_cross, to_chip)
        tiles, own = finish()
        total = own + from_cross.astype(f32) + from_chip.astype(f32)
        p_own = spread(total.astype(bf16))
        p_cross, p_chip = exchange(p_own, p_own)
        return tiles, p_own, p_cross, p_chip

    grad = pltpu.VMEM((both, wide), f32)
    mats = pltpu.VMEM((both, wide), bf16)
    nat = pltpu.VMEM((2, wide, count), bf16)
    ptq = pltpu.VMEM((2, both, count), bf16)
    four = shape((4, rows, width), f32)

    _, p_own, p_cross, p_chip = products(to_cross, to_chip, lambda: (None, own))
    mine, t_own, nat_own = call(
        functools.partial(own_kernel, blocks, False), [SMEM] + [VMEM] * 5,
        (shape((3, rows, width), f32), full, shape((wide, count), bf16)), [slots, grad, mats], 12 * unit, 4 << 20,
    )(coords, omega, turned, s_own, stq, p_own)
    outer, to_cross, to_chip = call(
        functools.partial(outer_kernel, blocks), [SMEM] + [VMEM] * 9,
        (four, part, part), [slots, nat, ptq, grad, mats, pltpu.VMEM((both, width), f32)], 36 * unit, 6 << 20,
    )(coords, omega, turned, s_before, s_own, s_after, stq, nat_own, p_cross, p_chip)

    def finish():
        return call(
            functools.partial(inner_kernel, blocks), [SMEM] + [VMEM] * 8,
            (four, full), [slots, nat, ptq, grad, mats], 12 * unit, 4 << 20,
        )(coords, omega, s_own, s_after, stq, p_own, p_cross, p_chip, t_own)

    inner, p_own, p_cross, p_chip = products(to_cross, to_chip, finish)
    whole = shape(omega.shape, f32)
    begun = call(
        functools.partial(own_kernel, blocks, True), [SMEM] + [VMEM] * 4, whole,
        [slots, grad, pltpu.VMEM((wide, count), bf16), pltpu.VMEM((3, rows, width), f32), pltpu.SemaphoreType.DMA((3,))],
        8 * unit, 3 << 20, out_specs=ANY,
    )(coords, mine, s_own, stq, p_own)
    return call(
        functools.partial(last_kernel, blocks), [SMEM] + [VMEM] * 7 + [ANY], whole,
        [slots, nat, ptq, pltpu.VMEM((2, both, wide), f32), pltpu.VMEM((8, rows, width), f32), pltpu.SemaphoreType.DMA((8,))],
        16 * unit, 6 << 20, aliases={8: 0}, out_specs=ANY,
    )(coords, outer, inner, s_after, stq, p_own, p_cross, p_chip, begun)


def solution(mesh):
    in_specs = (P("samp", "tiles"), P("tiles", "samp", None), P("tiles", None))
    out_specs = P("tiles", "samp", None)

    return jax.shard_map(shards, mesh=mesh, in_specs=in_specs, out_specs=out_specs, check_vma=False)
```

```python
import functools

import jax
import jax.numpy as jnp
from jax import lax
from jax.experimental import pallas as pl
from jax.experimental.pallas import tpu as pltpu
from jax.sharding import PartitionSpec as P


BLK_DEV = 2
step_size = 0.25
penalty = 0.2

VMEM = pl.BlockSpec(memory_space=pltpu.VMEM)
SMEM = pl.BlockSpec(memory_space=pltpu.SMEM)
ANY = pl.BlockSpec(memory_space=pl.ANY)
HBM = pl.BlockSpec(memory_space=pltpu.HBM)
bf16, f32 = jnp.bfloat16, jnp.float32

OWN_PAIR = 8
LIMIT = 12 << 20


def dot_nn(a, b):
    return jnp.dot(a, b, preferred_element_type=f32)


def dot_nt(a, b):
    return lax.dot_general(a, b, (((1,), (1,)), ((), ())), preferred_element_type=f32)


def shrink(value):
    level = step_size * penalty
    return value - jnp.clip(value, -level, level)


def shrink_diagonal(value, quarter):
    rows, width = value.shape
    row_ids = quarter * rows + lax.broadcasted_iota(jnp.int32, (rows, width), 0)
    col_ids = lax.broadcasted_iota(jnp.int32, (rows, width), 1)
    positive = 0.5 * (value + jnp.sqrt(value * value + 4.0 * step_size))
    return jnp.where(row_ids == col_ids, positive, shrink(value))


def find_slots(blocks, coords, slot_of):
    first = (lax.axis_index("tiles") - 1) * BLK_DEV
    for pair in range(OWN_PAIR + 1):
        slot_of[pair] = 0

    def place(slot, side):
        at = coords[slot, side] - first
        at = jnp.where(at < 0, at + blocks, at)
        return jnp.where(at >= blocks, at - blocks, at)

    for slot in range(BLK_DEV, coords.shape[0]):
        row, col = place(slot, 0), place(slot, 1)
        pair = jnp.where(col >= 2 * BLK_DEV, (col - 2 * BLK_DEV) * 2 * BLK_DEV + row, OWN_PAIR)
        slot_of[pair] = slot


def is_even():
    return lax.rem(lax.axis_index("tiles"), 2) == 0


def repeat_kernel(x, out, held, in_sem, out_sems):
    load = pltpu.make_async_copy(x, held, in_sem)
    load.start()
    load.wait()
    stores = [pltpu.make_async_copy(held, out.at[part], out_sems.at[part]) for part in range(out.shape[0])]
    for store in stores:
        store.start()
    for store in stores:
        store.wait()


def cut_kernel(omega, out, held, pieces, in_sems, out_sems):
    rows = omega.shape[1]
    others = held.shape[0]
    loads = [
        pltpu.make_async_copy(omega.at[BLK_DEV + k], held.at[k], in_sems.at[k]) for k in range(others)
    ]
    for load in loads:
        load.start()
    stores = []
    for k in range(others):
        loads[k].wait()
        for part in range(out.shape[0]):
            pieces[part, k] = held[k, :, part * rows : (part + 1) * rows].astype(bf16).T
        stores.append(pltpu.make_async_copy(pieces.at[:, k], out.at[:, k], out_sems.at[k]))
        stores[-1].start()
    for store in stores:
        store.wait()


def send_halves(cross, chip, before, after):
    @pl.when(is_even())
    def _():
        cross[...] = before
        chip[...] = after

    @pl.when(jnp.logical_not(is_even()))
    def _():
        cross[...] = after
        chip[...] = before


def begin_kernel(
    blocks, coords, omega, parts, s_own, s_cross, s_chip,
    s_before, s_after, turned, cross, chip, own, slot_of, mats, s_sems, t_sems,
):
    rows, width = omega.shape[1:]
    count = parts.shape[0]
    find_slots(blocks, coords, slot_of)
    even = is_even()

    def windows(before, after):
        return (
            pltpu.make_async_copy(before, s_before, s_sems.at[0]),
            pltpu.make_async_copy(after, s_after, s_sems.at[1]),
        )

    @pl.when(even)
    def _():
        for copy in windows(s_cross, s_chip):
            copy.start()

    @pl.when(jnp.logical_not(even))
    def _():
        for copy in windows(s_chip, s_cross):
            copy.start()

    def fill(pair):
        slot = slot_of[pair]
        unit = OWN_PAIR if pair == OWN_PAIR else pair % 4 * 2 + pair // 4
        copies = [
            pltpu.make_async_copy(
                parts.at[part, slot - BLK_DEV],
                turned.at[unit, :, part * rows : (part + 1) * rows],
                t_sems.at[pair, part],
            )
            for part in range(count)
        ]
        return slot, unit, copies

    for pair in range(OWN_PAIR + 1):
        slot, unit, copies = fill(pair)

        @pl.when(slot > 0)
        def _(copies=copies):
            for copy in copies:
                copy.start()

        @pl.when(slot == 0)
        def _(unit=unit):
            turned[unit] = jnp.zeros_like(turned[unit])

    def convert(pair, carry):
        slot = slot_of[pair]

        @pl.when(slot > 0)
        def _():
            mats[pair] = omega[slot].astype(bf16)

        @pl.when(slot == 0)
        def _():
            mats[pair] = jnp.zeros_like(mats[pair])

        return carry

    lax.fori_loop(0, OWN_PAIR + 1, convert, 0)
    left, right = s_own[:, :width], s_own[:, width:]
    own[:rows] = dot_nt(omega[0].astype(bf16), left) + dot_nt(mats[OWN_PAIR], right)
    own[rows:] = dot_nt(omega[1].astype(bf16), right)
    for copy in windows(s_chip, s_chip):
        copy.wait()
    total = dot_nt(mats[0:4].reshape(4 * rows, width), s_after[:, :width])
    total += dot_nt(mats[4:8].reshape(4 * rows, width), s_after[:, width:])
    own[...] += total[2 * rows :]
    for pair in range(OWN_PAIR + 1):
        slot, unit, copies = fill(pair)

        @pl.when(slot > 0)
        def _(copies=copies):
            for copy in copies:
                copy.wait()

    own[rows:] += dot_nt(turned[OWN_PAIR], left)
    after = jnp.zeros(own.shape, f32)
    for a in range(2 * BLK_DEV):
        source = (s_before, s_own)[a // BLK_DEV]
        blk = a % BLK_DEV
        after += dot_nt(turned[2 * a : 2 * a + 2].reshape(2 * rows, width), source[:, blk * width : (blk + 1) * width])
    send_halves(cross, chip, total[: 2 * rows].astype(bf16), after.astype(bf16))


def natural(out, pieces):
    count, both = pieces.shape[0], pieces.shape[1]
    rows = both // BLK_DEV
    for blk in range(BLK_DEV):
        for part in range(count):
            at = (blk * count + part) * rows
            out[at : at + rows, :] = pieces[part, blk * rows : (blk + 1) * rows, :]


def transpose_columns(stq, windows, quarter):
    rows = stq.shape[1] // BLK_DEV
    width = windows[0].shape[1] // BLK_DEV
    for side, ref in enumerate(windows):
        for blk in range(BLK_DEV):
            at = pl.multiple_of(blk * width + quarter * rows, rows)
            stq[side, blk * rows : (blk + 1) * rows, :] = ref[:, pl.ds(at, rows)].T


def own_kernel(
    blocks, coords, omega, turned, s_before, s_own, s_after, p_own,
    tiles, t_own, nat_own, stq, cols_half, rows_half, slot_of, grad, mats,
):
    rows, width = grad.shape[0] // 2, grad.shape[1] // 2
    quarter = lax.axis_index("samp")
    scale = step_size / (2.0 * s_own.shape[0])
    find_slots(blocks, coords, slot_of)
    transpose_columns(stq, (s_before, s_own, s_after), quarter)
    natural(nat_own, p_own)
    grad[...] = dot_nn(p_own[quarter], s_own[...]) + dot_nt(stq[1], nat_own[...])
    slot = slot_of[OWN_PAIR]
    for i in range(BLK_DEV):
        here = grad[i * rows : (i + 1) * rows, i * width : (i + 1) * width]
        tiles[i] = shrink_diagonal(omega[i] - scale * here, quarter)
    tiles[2] = shrink(omega[slot] - scale * grad[:rows, width:])
    mats[:rows, :width] = tiles[0].astype(bf16)
    mats[rows:, width:] = tiles[1].astype(bf16)

    @pl.when(slot > 0)
    def _():
        mats[:rows, width:] = tiles[2].astype(bf16)
        there = turned[OWN_PAIR].astype(f32) - scale * grad[rows:, :width]
        mats[rows:, :width] = shrink(there).astype(bf16)

    @pl.when(slot == 0)
    def _():
        mats[:rows, width:] = jnp.zeros((rows, width), bf16)
        mats[rows:, :width] = jnp.zeros((rows, width), bf16)

    t_own[...] = dot_nt(mats[...], s_own[...])
    cols_half[...] = dot_nt(stq[2], nat_own[...])
    rows_half[...] = dot_nn(p_own[quarter], s_after[...])


def own_last_kernel(
    blocks, coords, held, s_own, s_after, stq, p_own, out, rows_half, slot_of, grad, nat_own, tiles, sems,
):
    rows, width = grad.shape[0] // 2, grad.shape[1] // 2
    quarter = lax.axis_index("samp")
    scale = step_size / (2.0 * s_own.shape[0])
    find_slots(blocks, coords, slot_of)
    natural(nat_own, p_own)
    grad[...] = dot_nn(p_own[quarter], s_own[...]) + dot_nt(stq[1], nat_own[...])
    slot = slot_of[OWN_PAIR]
    copies = [pltpu.make_async_copy(tiles.at[i], out.at[i], sems.at[i]) for i in range(BLK_DEV)]
    copies.append(pltpu.make_async_copy(tiles.at[2], out.at[slot], sems.at[2]))
    for i in range(BLK_DEV):
        here = grad[i * rows : (i + 1) * rows, i * width : (i + 1) * width]
        tiles[i] = shrink_diagonal(held[i] - scale * here, quarter)
        copies[i].start()
    tiles[2] = shrink(held[2] - scale * grad[:rows, width:])

    @pl.when(slot > 0)
    def _():
        copies[2].start()

    rows_half[...] = dot_nn(p_own[quarter], s_after[...])
    for i in range(BLK_DEV):
        copies[i].wait()

    @pl.when(slot > 0)
    def _():
        copies[2].wait()


def order_halo(nat, ptq, p_cross, p_chip, quarter):
    even = is_even()
    for ref, at in ((p_cross, jnp.where(even, 0, 1)), (p_chip, jnp.where(even, 1, 0))):
        natural(nat.at[at], ref)
        ptq[at] = ref[quarter]


def update_rows(slot_of, source, grad, a_base, scale, tiles, mats):
    rows, width = grad.shape[0] // 2, grad.shape[1] // 2
    for a in range(2):
        for b in range(2):
            slot = slot_of[b * 4 + a_base + a]
            here = grad[a * rows : (a + 1) * rows, b * width : (b + 1) * width]
            tile = shrink(source[slot] - scale * here)
            tiles[a * 2 + b] = tile
            spot = (slice(a * rows, (a + 1) * rows), slice(b * width, (b + 1) * width))
            mats[spot] = jnp.where(slot > 0, tile, 0.0).astype(bf16)


def outer_kernel(
    blocks, coords, omega, turned, s_before, s_own, s_after, stq, cols_half, p_cross, p_chip,
    tiles, cross, chip, slot_of, nat, ptq, grad, mats, half,
):
    rows, width = omega.shape[1:]
    quarter = lax.axis_index("samp")
    scale = step_size / (2.0 * s_own.shape[0])
    find_slots(blocks, coords, slot_of)
    order_halo(nat, ptq, p_cross, p_chip, quarter)
    total = jnp.zeros(cross.shape, f32)
    for a in range(2 * BLK_DEV):
        blk = a % BLK_DEV
        at = slice(blk * width, (blk + 1) * width)
        source = (s_before, s_own)[a // BLK_DEV][:, at]
        other = dot_nt(stq[2], nat[0, at, :]) if a < BLK_DEV else cols_half[:, at]
        half[...] = dot_nn(ptq[1], source) + other
        for b in range(BLK_DEV):
            tile = shrink(turned[2 * a + b].astype(f32) - scale * half[b * rows : (b + 1) * rows, :])
            tile = jnp.where(slot_of[b * 4 + a] > 0, tile, 0.0)
            mats[b * rows : (b + 1) * rows, at] = tile.astype(bf16)
        total += dot_nt(mats[:, at], source)
    after = total.astype(bf16)
    grad[...] = dot_nn(ptq[0], s_after[...]) + dot_nt(stq[0], nat[1])
    update_rows(slot_of, omega, grad, 0, scale, tiles, mats)
    before = dot_nt(mats[...], s_after[...]).astype(bf16)
    send_halves(cross, chip, before, after)


def inner_kernel(
    blocks, coords, omega, s_own, s_after, stq, rows_half, p_cross, p_chip, t_own,
    tiles, own, slot_of, nat, ptq, grad, mats,
):
    quarter = lax.axis_index("samp")
    scale = step_size / (2.0 * s_own.shape[0])
    find_slots(blocks, coords, slot_of)
    order_halo(nat, ptq, p_cross, p_chip, quarter)
    grad[...] = rows_half[...] + dot_nt(stq[1], nat[1])
    update_rows(slot_of, omega, grad, BLK_DEV, scale, tiles, mats)
    own[...] = t_own[...] + dot_nt(mats[...], s_after[...])


def last_kernel(
    blocks, coords, outer, inner, s_after, stq, rows_half, p_cross, p_chip, begun,
    out, slot_of, nat, ptq, grad, tiles, sems,
):
    rows, width = tiles.shape[1:]
    quarter = lax.axis_index("samp")
    scale = step_size / (2.0 * s_after.shape[0])
    find_slots(blocks, coords, slot_of)
    order_halo(nat, ptq, p_cross, p_chip, quarter)
    for group in range(2):
        other = dot_nn(ptq[0], s_after[...]) if group == 0 else rows_half[...]
        grad[group] = other + dot_nt(stq[group], nat[1])
        for a in range(2):
            for b in range(2):
                unit = group * 4 + a * 2 + b
                slot = slot_of[b * 4 + group * 2 + a]
                here = grad[group, a * rows : (a + 1) * rows, b * width : (b + 1) * width]
                tiles[unit] = shrink((outer, inner)[group][a * 2 + b] - scale * here)

                @pl.when(slot > 0)
                def _(unit=unit, slot=slot):
                    pltpu.make_async_copy(tiles.at[unit], out.at[slot], sems.at[unit]).start()

    for group in range(2):
        for a in range(2):
            for b in range(2):
                unit = group * 4 + a * 2 + b
                slot = slot_of[b * 4 + group * 2 + a]

                @pl.when(slot > 0)
                def _(unit=unit, slot=slot):
                    pltpu.make_async_copy(tiles.at[unit], out.at[slot], sems.at[unit]).wait()


def shards(samples, omega, coords):
    size = lax.axis_size("tiles")
    parts = lax.axis_size("samp")
    blocks = BLK_DEV * size
    tiles, rows, width = omega.shape
    others = tiles - BLK_DEV
    count = samples.shape[0] * parts
    wide = samples.shape[1]
    both = BLK_DEV * rows
    chip = [(i, i ^ 1) for i in range(size)]
    cross = [(i, (i - 1) % size if i % 2 == 0 else (i + 1) % size) for i in range(size)]
    shape = jax.ShapeDtypeStruct
    slots = pltpu.SMEM((OWN_PAIR + 1,), jnp.int32)
    params = pltpu.CompilerParams(vmem_limit_bytes=LIMIT)

    def call(body, in_specs, outs, scratch, macs, moved, aliases=None, out_specs=None):
        several = isinstance(outs, tuple)
        specs = out_specs or ((VMEM,) * len(outs) if several else VMEM)
        return pl.pallas_call(
            body, out_shape=outs, in_specs=in_specs, out_specs=specs, scratch_shapes=scratch,
            compiler_params=params, input_output_aliases=aliases or {},
            cost_estimate=pl.CostEstimate(flops=2 * macs, bytes_accessed=moved, transcendentals=0),
        )

    def exchange(to_cross, to_chip):
        from_chip = lax.ppermute(to_chip, "tiles", chip)
        from_cross = lax.ppermute(to_cross, "tiles", cross)
        return from_cross, from_chip

    def spread(x):
        return lax.all_to_all(jnp.broadcast_to(x[None], (parts,) + x.shape), "samp", 0, 0)

    copies = call(
        repeat_kernel, [HBM], pltpu.HBM((parts,) + samples.shape, bf16),
        [pltpu.VMEM(samples.shape, bf16), pltpu.SemaphoreType.DMA, pltpu.SemaphoreType.DMA((parts,))],
        0, 1 << 20, out_specs=HBM,
    )(pltpu.with_memory_space_constraint(samples, pltpu.HBM))
    s_own = lax.all_to_all(copies, "samp", 0, 0).reshape(count, wide)
    pieces = call(
        cut_kernel, [HBM], pltpu.HBM((parts, others, rows, rows), bf16),
        [
            pltpu.VMEM((others, rows, width), f32), pltpu.VMEM((parts, others, rows, rows), bf16),
            pltpu.SemaphoreType.DMA((others,)), pltpu.SemaphoreType.DMA((others,)),
        ],
        0, 4 << 20, out_specs=HBM,
    )(pltpu.with_memory_space_constraint(omega, pltpu.HBM))
    turned_parts = lax.all_to_all(pieces, "samp", 0, 0)
    s_cross, s_chip = exchange(s_own, s_own)

    window = shape((count, wide), bf16)
    part = shape((both, count), bf16)
    full = shape((both, count), f32)
    unit = rows * width * count
    s_before, s_after, turned, to_cross, to_chip, own = call(
        functools.partial(begin_kernel, blocks), [SMEM, VMEM, ANY, VMEM, ANY, ANY],
        (window, window, shape((OWN_PAIR + 1, rows, width), bf16), part, part, full),
        [
            slots, pltpu.VMEM((OWN_PAIR + 1, rows, width), bf16),
            pltpu.SemaphoreType.DMA((2,)), pltpu.SemaphoreType.DMA((OWN_PAIR + 1, parts)),
        ],
        20 * unit, 6 << 20,
    )(coords, omega, turned_parts, s_own, s_cross, s_chip)

    def products(to_cross, to_chip, finish):
        from_cross, from_chip = exchange(to_cross, to_chip)
        tiles, own = finish()
        total = own + from_cross.astype(f32) + from_chip.astype(f32)
        p_own = spread(total.astype(bf16))
        p_cross, p_chip = exchange(p_own, p_own)
        return tiles, p_own, p_cross, p_chip

    grad = pltpu.VMEM((both, wide), f32)
    mats = pltpu.VMEM((both, wide), bf16)
    nat = pltpu.VMEM((2, wide, count), bf16)
    ptq = pltpu.VMEM((2, both, count), bf16)
    four = shape((4, rows, width), f32)

    _, p_own, p_cross, p_chip = products(to_cross, to_chip, lambda: (None, own))
    wide_half = shape((both, wide), f32)
    mine, t_own, _, stq, cols_half, rows_half = call(
        functools.partial(own_kernel, blocks), [SMEM] + [VMEM] * 6,
        (
            shape((3, rows, width), f32), full, shape((wide, count), bf16), shape((3, both, count), bf16),
            wide_half, wide_half,
        ),
        [slots, grad, mats], 20 * unit, 6 << 20,
    )(coords, omega, turned, s_before, s_own, s_after, p_own)
    outer, to_cross, to_chip = call(
        functools.partial(outer_kernel, blocks), [SMEM] + [VMEM] * 9,
        (four, part, part), [slots, nat, ptq, grad, mats, pltpu.VMEM((both, width), f32)], 32 * unit, 6 << 20,
    )(coords, omega, turned, s_before, s_own, s_after, stq, cols_half, p_cross, p_chip)

    def finish():
        return call(
            functools.partial(inner_kernel, blocks), [SMEM] + [VMEM] * 8,
            (four, full), [slots, nat, ptq, grad, mats], 8 * unit, 4 << 20,
        )(coords, omega, s_own, s_after, stq, rows_half, p_cross, p_chip, t_own)

    inner, p_own, p_cross, p_chip = products(to_cross, to_chip, finish)
    whole = shape(omega.shape, f32)
    begun, rows_half = call(
        functools.partial(own_last_kernel, blocks), [SMEM] + [VMEM] * 5, (whole, wide_half),
        [slots, grad, pltpu.VMEM((wide, count), bf16), pltpu.VMEM((3, rows, width), f32), pltpu.SemaphoreType.DMA((3,))],
        12 * unit, 3 << 20, out_specs=(ANY, VMEM),
    )(coords, mine, s_own, s_after, stq, p_own)
    return call(
        functools.partial(last_kernel, blocks), [SMEM] + [VMEM] * 7 + [ANY], whole,
        [slots, nat, ptq, pltpu.VMEM((2, both, wide), f32), pltpu.VMEM((8, rows, width), f32), pltpu.SemaphoreType.DMA((8,))],
        12 * unit, 6 << 20, aliases={8: 0}, out_specs=ANY,
    )(coords, outer, inner, s_after, stq, rows_half, p_cross, p_chip, begun)


def solution(mesh):
    in_specs = (P("samp", "tiles"), P("tiles", "samp", None), P("tiles", None))
    out_specs = P("tiles", "samp", None)

    return jax.shard_map(shards, mesh=mesh, in_specs=in_specs, out_specs=out_specs, check_vma=False)
```

```python
import functools

import jax
import jax.numpy as jnp
from jax import lax
from jax.experimental import pallas as pl
from jax.experimental.pallas import tpu as pltpu
from jax.sharding import PartitionSpec as P


BLK_DEV = 2
step_size = 0.25
penalty = 0.2

VMEM = pl.BlockSpec(memory_space=pltpu.VMEM)
SMEM = pl.BlockSpec(memory_space=pltpu.SMEM)
ANY = pl.BlockSpec(memory_space=pl.ANY)
HBM = pl.BlockSpec(memory_space=pltpu.HBM)
bf16, f32 = jnp.bfloat16, jnp.float32

OWN_PAIR = 8
LIMIT = 12 << 20


def dot_nn(a, b):
    return jnp.dot(a, b, preferred_element_type=f32)


def dot_nt(a, b):
    return lax.dot_general(a, b, (((1,), (1,)), ((), ())), preferred_element_type=f32)


def shrink(value):
    level = step_size * penalty
    return value - jnp.clip(value, -level, level)


def shrink_diagonal(value, quarter):
    rows, width = value.shape
    row_ids = quarter * rows + lax.broadcasted_iota(jnp.int32, (rows, width), 0)
    col_ids = lax.broadcasted_iota(jnp.int32, (rows, width), 1)
    positive = 0.5 * (value + jnp.sqrt(value * value + 4.0 * step_size))
    return jnp.where(row_ids == col_ids, positive, shrink(value))


def find_slots(blocks, coords, slot_of):
    first = (lax.axis_index("tiles") - 1) * BLK_DEV
    for pair in range(OWN_PAIR + 1):
        slot_of[pair] = 0

    def place(slot, side):
        at = coords[slot, side] - first
        at = jnp.where(at < 0, at + blocks, at)
        return jnp.where(at >= blocks, at - blocks, at)

    for slot in range(BLK_DEV, coords.shape[0]):
        row, col = place(slot, 0), place(slot, 1)
        pair = jnp.where(col >= 2 * BLK_DEV, (col - 2 * BLK_DEV) * 2 * BLK_DEV + row, OWN_PAIR)
        slot_of[pair] = slot


def is_even():
    return lax.rem(lax.axis_index("tiles"), 2) == 0


def repeat_kernel(x, out, held, in_sem, out_sems):
    load = pltpu.make_async_copy(x, held, in_sem)
    load.start()
    load.wait()
    stores = [pltpu.make_async_copy(held, out.at[part], out_sems.at[part]) for part in range(out.shape[0])]
    for store in stores:
        store.start()
    for store in stores:
        store.wait()


def cut_kernel(omega, out, held, pieces, in_sems, out_sems):
    rows = omega.shape[1]
    others = held.shape[0]
    loads = [
        pltpu.make_async_copy(omega.at[BLK_DEV + k], held.at[k], in_sems.at[k]) for k in range(others)
    ]
    for load in loads:
        load.start()
    stores = []
    for k in range(others):
        loads[k].wait()
        for part in range(out.shape[0]):
            pieces[part, k] = held[k, :, part * rows : (part + 1) * rows].astype(bf16).T
        stores.append(pltpu.make_async_copy(pieces.at[:, k], out.at[:, k], out_sems.at[k]))
        stores[-1].start()
    for store in stores:
        store.wait()


def choose(even_is_first, first, second):
    even = is_even()

    @pl.when(even if even_is_first else jnp.logical_not(even))
    def _():
        first()

    @pl.when(jnp.logical_not(even) if even_is_first else even)
    def _():
        second()


def next_side():
    return jnp.where(is_even(), 2, 0)


def put_tile(slot, tile, mats, at):
    mats[at] = jnp.where(slot > 0, tile, 0.0).astype(bf16)


def spot(i, rows, start, width):
    return slice(i * rows, (i + 1) * rows), slice(start, start + width)


def first_rows(slot_of, omega, base, s_near, mats):
    rows, width = omega.shape[1:]
    for i in range(2):
        for blk in range(2):
            slot = slot_of[blk * 4 + base + i]
            put_tile(slot, omega[slot], mats, spot(i, rows, blk * width, width))
    return dot_nt(mats[...], s_near[...])


def first_cols(turned, s_near, s_own):
    rows, width = turned.shape[1:]
    total = jnp.zeros((2 * rows, s_own.shape[0]), f32)
    for a in range(2 * BLK_DEV):
        source = (s_near, s_own)[a // BLK_DEV]
        blk = a % BLK_DEV
        total += dot_nt(turned[2 * a : 2 * a + 2].reshape(2 * rows, width), source[:, blk * width : (blk + 1) * width])
    return total


def first_cross_kernel(blocks, coords, omega, parts, s_own, s_chip, turned, out, slot_of, mats, sems):
    rows, _ = omega.shape[1:]
    count = parts.shape[0]
    find_slots(blocks, coords, slot_of)

    def fill(pair):
        slot = slot_of[pair]
        unit = OWN_PAIR if pair == OWN_PAIR else pair % 4 * 2 + pair // 4
        copies = [
            pltpu.make_async_copy(
                parts.at[part, slot - BLK_DEV],
                turned.at[unit, :, part * rows : (part + 1) * rows],
                sems.at[pair, part],
            )
            for part in range(count)
        ]
        return slot, unit, copies

    for pair in range(OWN_PAIR + 1):
        slot, unit, copies = fill(pair)

        @pl.when(slot > 0)
        def _(copies=copies):
            for copy in copies:
                copy.start()

        @pl.when(slot == 0)
        def _(unit=unit):
            turned[unit] = jnp.zeros_like(turned[unit])

    @pl.when(is_even())
    def _():
        out[...] = first_rows(slot_of, omega, 0, s_chip, mats).astype(bf16)

    for pair in range(OWN_PAIR + 1):
        slot, unit, copies = fill(pair)

        @pl.when(slot > 0)
        def _(copies=copies):
            for copy in copies:
                copy.wait()

    @pl.when(jnp.logical_not(is_even()))
    def _():
        out[...] = first_cols(turned, s_chip, s_own).astype(bf16)


def first_chip_kernel(blocks, coords, omega, turned, s_own, s_cross, out, slot_of, mats):
    find_slots(blocks, coords, slot_of)

    def cols():
        out[...] = first_cols(turned, s_cross, s_own).astype(bf16)

    def rows():
        out[...] = first_rows(slot_of, omega, 0, s_cross, mats).astype(bf16)

    choose(True, cols, rows)


def first_own_kernel(blocks, coords, omega, turned, s_own, s_cross, s_chip, own, stq, slot_of, mats):
    rows, width = omega.shape[1:]
    quarter = lax.axis_index("samp")
    find_slots(blocks, coords, slot_of)
    mats[:rows, :width] = omega[0].astype(bf16)
    mats[rows:, width:] = omega[1].astype(bf16)
    slot = slot_of[OWN_PAIR]
    put_tile(slot, omega[slot], mats, spot(0, rows, width, width))
    mats[rows:, :width] = turned[OWN_PAIR]
    own[...] = dot_nt(mats[...], s_own[...])

    def add(s_next):
        own[...] += first_rows(slot_of, omega, BLK_DEV, s_next, mats)

    choose(True, lambda: add(s_chip), lambda: add(s_cross))
    for side, ref in enumerate((s_cross, s_own, s_chip)):
        for blk in range(BLK_DEV):
            at = pl.multiple_of(blk * width + quarter * rows, rows)
            stq[side, blk * rows : (blk + 1) * rows, :] = ref[:, pl.ds(at, rows)].T


def half_kernel(stq, p_own, out):
    count, both = p_own.shape[0], p_own.shape[1]
    rows = both // BLK_DEV
    far = stq[next_side()]
    for part in range(count):
        piece = dot_nt(far, p_own[part])
        for blk in range(BLK_DEV):
            at = (blk * count + part) * rows
            out[:, at : at + rows] = piece[:, blk * rows : (blk + 1) * rows]


def update_edge(old, slots, ptq, far, s_near, p_near, scale, grad, put):
    count, both = p_near.shape[0], p_near.shape[1]
    rows = both // BLK_DEV
    grad[...] = dot_nn(ptq, s_near[...])
    for part in range(count):
        piece = dot_nt(far, p_near[part])
        for i in range(2):
            for blk in range(2):
                at = spot(i, rows, (blk * count + part) * rows, rows)
                here = grad[at] + piece[i * rows : (i + 1) * rows, blk * rows : (blk + 1) * rows]
                slot = slots(i, blk)
                put(i, blk, part, slot, shrink(old(i, blk, part, slot) - scale * here))


def edge_kernel(
    blocks, far_side, coords, omega, turned, s_own, s_near, p_near, p_far, stq, own_half,
    tiles, out, slot_of, grad, mats,
):
    rows, width = omega.shape[1:]
    wide = s_own.shape[1]
    quarter = lax.axis_index("samp")
    scale = step_size / (2.0 * s_own.shape[0])
    find_slots(blocks, coords, slot_of)

    def columns(part):
        return slice(part * rows, (part + 1) * rows)

    def far_rows():
        return p_far[quarter] if far_side else p_far[...]

    def row_tiles():
        def put(i, blk, part, slot, tile):
            tiles[i * 2 + blk, :, columns(part)] = tile
            put_tile(slot, tile, mats, spot(i, rows, blk * width + part * rows, rows))

        update_edge(
            lambda i, blk, part, slot: omega[slot, :, columns(part)], lambda i, blk: slot_of[blk * 4 + i],
            far_rows(), stq[far_side], s_near, p_near, scale, grad, put,
        )
        out[...] = dot_nt(mats[:, :wide], s_near[...]).astype(bf16)

    def col_tiles():
        def put(i, blk, part, slot, tile):
            put_tile(slot, tile, mats, spot(i, rows, blk * width + part * rows, rows))

        update_edge(
            lambda i, blk, part, slot: turned[2 * blk + i, :, columns(part)].astype(f32),
            lambda i, blk: slot_of[i * 4 + blk],
            far_rows(), stq[far_side], s_near, p_near, scale, grad, put,
        )
        grad[...] = dot_nn(far_rows(), s_own[...]) + own_half[...]
        for i in range(2):
            for blk in range(2):
                tile = turned[2 * (BLK_DEV + blk) + i].astype(f32) - scale * grad[spot(i, rows, blk * width, width)]
                put_tile(slot_of[i * 4 + BLK_DEV + blk], shrink(tile), mats, spot(i, rows, wide + blk * width, width))
        total = dot_nt(mats[:, :wide], s_near[...]) + dot_nt(mats[:, wide:], s_own[...])
        out[...] = total.astype(bf16)

    choose(far_side == 0, row_tiles, col_tiles)


def natural(out, pieces):
    count, both = pieces.shape[0], pieces.shape[1]
    rows = both // BLK_DEV
    for blk in range(BLK_DEV):
        for part in range(count):
            at = (blk * count + part) * rows
            out[at : at + rows, :] = pieces[part, blk * rows : (blk + 1) * rows, :]


def own_kernel(blocks, coords, omega, turned, s_own, stq, p_own, tiles, t_own, slot_of, grad, mats, nat_own):
    rows, width = grad.shape[0] // 2, grad.shape[1] // 2
    quarter = lax.axis_index("samp")
    scale = step_size / (2.0 * s_own.shape[0])
    find_slots(blocks, coords, slot_of)
    natural(nat_own, p_own)
    grad[...] = dot_nn(p_own[quarter], s_own[...]) + dot_nt(stq[1], nat_own[...])
    slot = slot_of[OWN_PAIR]
    for i in range(BLK_DEV):
        here = grad[spot(i, rows, i * width, width)]
        tiles[i] = shrink_diagonal(omega[i] - scale * here, quarter)
        mats[spot(i, rows, i * width, width)] = tiles[i].astype(bf16)
    tiles[2] = shrink(omega[slot] - scale * grad[:rows, width:])
    put_tile(slot, tiles[2], mats, spot(0, rows, width, width))
    there = turned[OWN_PAIR].astype(f32) - scale * grad[rows:, :width]
    put_tile(slot, shrink(there), mats, spot(1, rows, 0, width))
    t_own[...] = dot_nt(mats[...], s_own[...])


def inner_kernel(
    blocks, coords, omega, s_cross, s_chip, stq, p_own, p_cross, p_chip, t_own, tiles, own, slot_of, grad, mats
):
    rows, width = omega.shape[1:]
    quarter = lax.axis_index("samp")
    scale = step_size / (2.0 * s_chip.shape[0])
    find_slots(blocks, coords, slot_of)

    def put(i, blk, part, slot, tile):
        tiles[i * 2 + blk, :, part * rows : (part + 1) * rows] = tile
        put_tile(slot, tile, mats, spot(i, rows, blk * width + part * rows, rows))

    def run(s_next, p_next):
        update_edge(
            lambda i, blk, part, slot: omega[slot, :, part * rows : (part + 1) * rows],
            lambda i, blk: slot_of[blk * 4 + BLK_DEV + i],
            p_own[quarter], stq[1], s_next, p_next, scale, grad, put,
        )
        own[...] = t_own[...] + dot_nt(mats[...], s_next[...])

    choose(True, lambda: run(s_chip, p_chip), lambda: run(s_cross, p_cross))


def own_last_kernel(
    blocks, coords, held, s_own, s_cross, s_chip, stq, p_own, out, rows_half, slot_of, grad, nat_own, tiles, sems,
):
    rows, width = grad.shape[0] // 2, grad.shape[1] // 2
    quarter = lax.axis_index("samp")
    scale = step_size / (2.0 * s_own.shape[0])
    find_slots(blocks, coords, slot_of)
    natural(nat_own, p_own)
    grad[...] = dot_nn(p_own[quarter], s_own[...]) + dot_nt(stq[1], nat_own[...])
    slot = slot_of[OWN_PAIR]
    copies = [pltpu.make_async_copy(tiles.at[i], out.at[i], sems.at[i]) for i in range(BLK_DEV)]
    copies.append(pltpu.make_async_copy(tiles.at[2], out.at[slot], sems.at[2]))
    for i in range(BLK_DEV):
        here = grad[i * rows : (i + 1) * rows, i * width : (i + 1) * width]
        tiles[i] = shrink_diagonal(held[i] - scale * here, quarter)
        copies[i].start()
    tiles[2] = shrink(held[2] - scale * grad[:rows, width:])

    @pl.when(slot > 0)
    def _():
        copies[2].start()

    def half(s_next):
        rows_half[...] = dot_nn(p_own[quarter], s_next[...])

    choose(True, lambda: half(s_chip), lambda: half(s_cross))
    for i in range(BLK_DEV):
        copies[i].wait()

    @pl.when(slot > 0)
    def _():
        copies[2].wait()


def last_kernel(
    blocks, coords, outer_cross, outer_chip, inner, s_cross, s_chip, stq, rows_half, p_cross, p_chip, begun,
    out, slot_of, grad, tiles, sems,
):
    rows, _ = tiles.shape[1:]
    quarter = lax.axis_index("samp")
    count = p_chip.shape[0]
    scale = step_size / (2.0 * s_chip.shape[0])
    find_slots(blocks, coords, slot_of)

    def copy(unit, slot):
        return pltpu.make_async_copy(tiles.at[unit], out.at[slot], sems.at[unit])

    def slot_at(group, i, blk):
        return slot_of[blk * 4 + group * BLK_DEV + i]

    def run(outer, s_next, p_next, p_far, far):
        grad[...] = dot_nn(p_far[quarter], s_next[...])
        for group in (1, 0):
            rest = (grad, rows_half)[group]
            for part in range(count):
                piece = dot_nt((far, stq[1])[group], p_next[part])
                for i in range(2):
                    for blk in range(2):
                        at = spot(i, rows, (blk * count + part) * rows, rows)
                        here = rest[at] + piece[i * rows : (i + 1) * rows, blk * rows : (blk + 1) * rows]
                        cols = slice(part * rows, (part + 1) * rows)
                        old = (outer, inner)[group][i * 2 + blk, :, cols]
                        tiles[group * 4 + i * 2 + blk, :, cols] = shrink(old - scale * here)
            for i in range(2):
                for blk in range(2):
                    unit, slot = group * 4 + i * 2 + blk, slot_at(group, i, blk)

                    @pl.when(slot > 0)
                    def _(unit=unit, slot=slot):
                        copy(unit, slot).start()

    choose(
        True,
        lambda: run(outer_cross, s_chip, p_chip, p_cross, stq[0]),
        lambda: run(outer_chip, s_cross, p_cross, p_chip, stq[2]),
    )
    for group in range(2):
        for i in range(2):
            for blk in range(2):
                unit, slot = group * 4 + i * 2 + blk, slot_at(group, i, blk)

                @pl.when(slot > 0)
                def _(unit=unit, slot=slot):
                    copy(unit, slot).wait()


def shards(samples, omega, coords):
    size = lax.axis_size("tiles")
    parts = lax.axis_size("samp")
    blocks = BLK_DEV * size
    tiles, rows, width = omega.shape
    others = tiles - BLK_DEV
    count = samples.shape[0] * parts
    wide = samples.shape[1]
    both = BLK_DEV * rows
    chip = [(i, i ^ 1) for i in range(size)]
    cross = [(i, (i - 1) % size if i % 2 == 0 else (i + 1) % size) for i in range(size)]
    shape = jax.ShapeDtypeStruct
    slots = pltpu.SMEM((OWN_PAIR + 1,), jnp.int32)
    params = pltpu.CompilerParams(vmem_limit_bytes=LIMIT)

    def call(body, in_specs, outs, scratch, macs, moved, aliases=None, out_specs=None):
        several = isinstance(outs, tuple)
        specs = out_specs or ((VMEM,) * len(outs) if several else VMEM)
        return pl.pallas_call(
            body, out_shape=outs, in_specs=in_specs, out_specs=specs, scratch_shapes=scratch,
            compiler_params=params, input_output_aliases=aliases or {},
            cost_estimate=pl.CostEstimate(flops=2 * macs, bytes_accessed=moved, transcendentals=0),
        )

    def permute(x, pairs):
        return lax.ppermute(x, "tiles", pairs)

    def spread(x):
        return lax.all_to_all(jnp.broadcast_to(x[None], (parts,) + x.shape), "samp", 0, 0)

    copies = call(
        repeat_kernel, [HBM], pltpu.HBM((parts,) + samples.shape, bf16),
        [pltpu.VMEM(samples.shape, bf16), pltpu.SemaphoreType.DMA, pltpu.SemaphoreType.DMA((parts,))],
        0, 1 << 20, out_specs=HBM,
    )(pltpu.with_memory_space_constraint(samples, pltpu.HBM))
    s_own = lax.all_to_all(copies, "samp", 0, 0).reshape(count, wide)
    pieces = call(
        cut_kernel, [HBM], pltpu.HBM((parts, others, rows, rows), bf16),
        [
            pltpu.VMEM((others, rows, width), f32), pltpu.VMEM((parts, others, rows, rows), bf16),
            pltpu.SemaphoreType.DMA((others,)), pltpu.SemaphoreType.DMA((others,)),
        ],
        0, 4 << 20, out_specs=HBM,
    )(pltpu.with_memory_space_constraint(omega, pltpu.HBM))
    turned_parts = lax.all_to_all(pieces, "samp", 0, 0)
    s_cross = permute(s_own, cross)
    s_chip = permute(s_own, chip)

    part = shape((both, count), bf16)
    full = shape((both, count), f32)
    four = shape((4, rows, width), f32)
    wide_half = shape((both, wide), f32)
    unit = rows * width * count
    grad = pltpu.VMEM((both, wide), f32)
    mats = pltpu.VMEM((both, wide), bf16)
    mats_two = pltpu.VMEM((both, 2 * wide), bf16)
    nat = pltpu.VMEM((wide, count), bf16)

    def run(body, args, in_specs, outs, scratch, units, out_specs=None, aliases=None):
        return call(body, in_specs, outs, scratch, units * unit, 4 << 20, aliases, out_specs)(*args)

    def kernel(body, *extra):
        return functools.partial(body, blocks, *extra)

    turned, to_cross = run(
        kernel(first_cross_kernel), (coords, omega, turned_parts, s_own, s_chip), [SMEM, VMEM, ANY, VMEM, VMEM],
        (shape((OWN_PAIR + 1, rows, width), bf16), part),
        [slots, mats, pltpu.SemaphoreType.DMA((OWN_PAIR + 1, parts))], 8,
    )
    from_cross = permute(to_cross, cross)
    to_chip = run(
        kernel(first_chip_kernel), (coords, omega, turned, s_own, s_cross), [SMEM] + [VMEM] * 4,
        part, [slots, mats], 8,
    )
    from_chip = permute(to_chip, chip)
    own, stq = run(
        kernel(first_own_kernel), (coords, omega, turned, s_own, s_cross, s_chip), [SMEM] + [VMEM] * 5,
        (full, shape((3, both, count), bf16)), [slots, mats], 8,
    )
    total = (own + from_cross.astype(f32) + from_chip.astype(f32)).astype(bf16)
    far_cross = permute(total, cross)
    p_own = spread(total)
    p_cross = permute(p_own, cross)
    p_chip = permute(p_own, chip)
    own_half = run(half_kernel, (stq, p_own), [VMEM] * 2, wide_half, [], 4)

    def edge(side, s_near, p_near, p_far):
        return run(
            kernel(edge_kernel, side), (coords, omega, turned, s_own, s_near, p_near, p_far, stq, own_half),
            [SMEM] + [VMEM] * 8, (four, part), [slots, grad, mats_two], 20,
        )

    outer_cross, to_cross = edge(0, s_chip, p_chip, far_cross)
    from_cross = permute(to_cross, cross)
    mine, t_own = run(
        kernel(own_kernel), (coords, omega, turned, s_own, stq, p_own), [SMEM] + [VMEM] * 5,
        (shape((3, rows, width), f32), full), [slots, grad, mats, nat], 12,
    )
    outer_chip, to_chip = edge(2, s_cross, p_cross, p_chip)
    from_chip = permute(to_chip, chip)
    inner, own = run(
        kernel(inner_kernel), (coords, omega, s_cross, s_chip, stq, p_own, p_cross, p_chip, t_own),
        [SMEM] + [VMEM] * 8, (four, full), [slots, grad, mats], 12,
    )
    total = (own + from_cross.astype(f32) + from_chip.astype(f32)).astype(bf16)
    p_own = spread(total)
    p_cross = permute(p_own, cross)
    p_chip = permute(p_own, chip)
    whole = shape(omega.shape, f32)
    begun, rows_half = run(
        kernel(own_last_kernel), (coords, mine, s_own, s_cross, s_chip, stq, p_own), [SMEM] + [VMEM] * 6,
        (whole, wide_half),
        [slots, grad, nat, pltpu.VMEM((3, rows, width), f32), pltpu.SemaphoreType.DMA((3,))],
        12, out_specs=(ANY, VMEM),
    )
    return run(
        kernel(last_kernel),
        (coords, outer_cross, outer_chip, inner, s_cross, s_chip, stq, rows_half, p_cross, p_chip, begun),
        [SMEM] + [VMEM] * 9 + [ANY], whole,
        [slots, grad, pltpu.VMEM((8, rows, width), f32), pltpu.SemaphoreType.DMA((8,))],
        12, out_specs=ANY, aliases={10: 0},
    )


def solution(mesh):
    in_specs = (P("samp", "tiles"), P("tiles", "samp", None), P("tiles", None))
    out_specs = P("tiles", "samp", None)

    return jax.shard_map(shards, mesh=mesh, in_specs=in_specs, out_specs=out_specs, check_vma=False)
```

```python
import functools

import jax
import jax.numpy as jnp
from jax import lax
from jax.experimental import pallas as pl
from jax.experimental.pallas import tpu as pltpu
from jax.sharding import PartitionSpec as P


BLK_DEV = 2
step_size = 0.25
penalty = 0.2

VMEM = pl.BlockSpec(memory_space=pltpu.VMEM)
SMEM = pl.BlockSpec(memory_space=pltpu.SMEM)
ANY = pl.BlockSpec(memory_space=pl.ANY)
HBM = pl.BlockSpec(memory_space=pltpu.HBM)
bf16, f32 = jnp.bfloat16, jnp.float32

OWN_PAIR = 8
LIMIT = 12 << 20


def dot_nn(a, b):
    return jnp.dot(a, b, preferred_element_type=f32)


def dot_nt(a, b):
    return lax.dot_general(a, b, (((1,), (1,)), ((), ())), preferred_element_type=f32)


def shrink(value):
    level = step_size * penalty
    return value - jnp.clip(value, -level, level)


def shrink_diagonal(value, quarter):
    rows, width = value.shape
    row_ids = quarter * rows + lax.broadcasted_iota(jnp.int32, (rows, width), 0)
    col_ids = lax.broadcasted_iota(jnp.int32, (rows, width), 1)
    positive = 0.5 * (value + jnp.sqrt(value * value + 4.0 * step_size))
    return jnp.where(row_ids == col_ids, positive, shrink(value))


def find_slots(blocks, coords, slot_of):
    first = (lax.axis_index("tiles") - 1) * BLK_DEV
    for pair in range(OWN_PAIR + 1):
        slot_of[pair] = 0

    def place(slot, side):
        at = coords[slot, side] - first
        at = jnp.where(at < 0, at + blocks, at)
        return jnp.where(at >= blocks, at - blocks, at)

    for slot in range(BLK_DEV, coords.shape[0]):
        row, col = place(slot, 0), place(slot, 1)
        pair = jnp.where(col >= 2 * BLK_DEV, (col - 2 * BLK_DEV) * 2 * BLK_DEV + row, OWN_PAIR)
        slot_of[pair] = slot


def is_even():
    return lax.rem(lax.axis_index("tiles"), 2) == 0


def prepare_kernel(x, omega, copies, out, held, pieces, x_held, x_sem, in_sems, out_sems):
    rows = omega.shape[1]
    others = held.shape[0]
    x_load = pltpu.make_async_copy(x, x_held, x_sem)
    x_load.start()
    loads = [
        pltpu.make_async_copy(omega.at[BLK_DEV + k], held.at[k], in_sems.at[k]) for k in range(others)
    ]
    for load in loads:
        load.start()
    x_load.wait()
    for part in range(copies.shape[0]):
        copies[part] = x_held[...]
    stores = []
    for k in range(others):
        loads[k].wait()
        for part in range(out.shape[0]):
            pieces[part, k] = held[k, :, part * rows : (part + 1) * rows].astype(bf16).T
        stores.append(pltpu.make_async_copy(pieces.at[:, k], out.at[:, k], out_sems.at[k]))
        stores[-1].start()
    for store in stores:
        store.wait()


def send_halves(cross, chip, before, after):
    @pl.when(is_even())
    def _():
        cross[...] = before
        chip[...] = after

    @pl.when(jnp.logical_not(is_even()))
    def _():
        cross[...] = after
        chip[...] = before


def begin_kernel(
    blocks, coords, omega, parts, s_own, s_cross, s_chip,
    s_before, s_after, turned, cross, chip, own, slot_of, mats, parts_held, s_sems, t_sem,
):
    rows, width = omega.shape[1:]
    count = parts.shape[0]
    find_slots(blocks, coords, slot_of)
    even = is_even()

    def windows(before, after):
        return (
            pltpu.make_async_copy(before, s_before, s_sems.at[0]),
            pltpu.make_async_copy(after, s_after, s_sems.at[1]),
        )

    @pl.when(even)
    def _():
        for copy in windows(s_cross, s_chip):
            copy.start()

    @pl.when(jnp.logical_not(even))
    def _():
        for copy in windows(s_chip, s_cross):
            copy.start()

    parts_copy = pltpu.make_async_copy(parts, parts_held, t_sem)
    parts_copy.start()

    def convert(pair, carry):
        slot = slot_of[pair]

        @pl.when(slot > 0)
        def _():
            mats[pair] = omega[slot].astype(bf16)

        @pl.when(slot == 0)
        def _():
            mats[pair] = jnp.zeros_like(mats[pair])

        return carry

    lax.fori_loop(0, OWN_PAIR + 1, convert, 0)
    left, right = s_own[:, :width], s_own[:, width:]
    own[:rows] = dot_nt(omega[0].astype(bf16), left) + dot_nt(mats[OWN_PAIR], right)
    own[rows:] = dot_nt(omega[1].astype(bf16), right)
    for copy in windows(s_chip, s_chip):
        copy.wait()
    total = dot_nt(mats[0:4].reshape(4 * rows, width), s_after[:, :width])
    total += dot_nt(mats[4:8].reshape(4 * rows, width), s_after[:, width:])
    own[...] += total[2 * rows :]
    parts_copy.wait()
    for pair in range(OWN_PAIR + 1):
        slot = slot_of[pair]
        unit = OWN_PAIR if pair == OWN_PAIR else pair % 4 * 2 + pair // 4
        for part in range(count):
            block = parts_held[part, jnp.maximum(slot - BLK_DEV, 0)]
            turned[unit, :, part * rows : (part + 1) * rows] = jnp.where(slot > 0, block, jnp.zeros_like(block))

    own[rows:] += dot_nt(turned[OWN_PAIR], left)
    after = jnp.zeros(own.shape, f32)
    for a in range(2 * BLK_DEV):
        source = (s_before, s_own)[a // BLK_DEV]
        blk = a % BLK_DEV
        after += dot_nt(turned[2 * a : 2 * a + 2].reshape(2 * rows, width), source[:, blk * width : (blk + 1) * width])
    send_halves(cross, chip, total[: 2 * rows].astype(bf16), after.astype(bf16))


def natural(out, pieces):
    count, both = pieces.shape[0], pieces.shape[1]
    rows = both // BLK_DEV
    for blk in range(BLK_DEV):
        for part in range(count):
            at = (blk * count + part) * rows
            out[at : at + rows, :] = pieces[part, blk * rows : (blk + 1) * rows, :]


def transpose_columns(stq, windows, quarter):
    rows = stq.shape[1] // BLK_DEV
    width = windows[0].shape[1] // BLK_DEV
    for side, ref in enumerate(windows):
        for blk in range(BLK_DEV):
            at = pl.multiple_of(blk * width + quarter * rows, rows)
            stq[side, blk * rows : (blk + 1) * rows, :] = ref[:, pl.ds(at, rows)].T


def own_kernel(
    slot_of, omega, turned, s_before, s_own, s_after, p_own,
    tiles, t_own, nat_own, stq, cols_half, rows_half, grad, mats,
):
    rows, width = grad.shape[0] // 2, grad.shape[1] // 2
    quarter = lax.axis_index("samp")
    scale = step_size / (2.0 * s_own.shape[0])
    transpose_columns(stq, (s_before, s_own, s_after), quarter)
    natural(nat_own, p_own)
    grad[...] = dot_nn(p_own[quarter], s_own[...]) + dot_nt(stq[1], nat_own[...])
    slot = slot_of[OWN_PAIR]
    for i in range(BLK_DEV):
        here = grad[i * rows : (i + 1) * rows, i * width : (i + 1) * width]
        tiles[i] = shrink_diagonal(omega[i] - scale * here, quarter)
    tiles[2] = shrink(omega[slot] - scale * grad[:rows, width:])
    mats[:rows, :width] = tiles[0].astype(bf16)
    mats[rows:, width:] = tiles[1].astype(bf16)

    @pl.when(slot > 0)
    def _():
        mats[:rows, width:] = tiles[2].astype(bf16)
        there = turned[OWN_PAIR].astype(f32) - scale * grad[rows:, :width]
        mats[rows:, :width] = shrink(there).astype(bf16)

    @pl.when(slot == 0)
    def _():
        mats[:rows, width:] = jnp.zeros((rows, width), bf16)
        mats[rows:, :width] = jnp.zeros((rows, width), bf16)

    t_own[...] = dot_nt(mats[...], s_own[...])
    cols_half[...] = dot_nt(stq[2], nat_own[...])
    rows_half[...] = dot_nn(p_own[quarter], s_after[...])


def own_last_kernel(
    slot_of, held, s_own, s_after, stq, p_own, out, rows_half, grad, nat_own, tiles, sems,
):
    rows, width = grad.shape[0] // 2, grad.shape[1] // 2
    quarter = lax.axis_index("samp")
    scale = step_size / (2.0 * s_own.shape[0])
    natural(nat_own, p_own)
    grad[...] = dot_nn(p_own[quarter], s_own[...]) + dot_nt(stq[1], nat_own[...])
    slot = slot_of[OWN_PAIR]
    copies = [pltpu.make_async_copy(tiles.at[i], out.at[i], sems.at[i]) for i in range(BLK_DEV)]
    copies.append(pltpu.make_async_copy(tiles.at[2], out.at[slot], sems.at[2]))
    for i in range(BLK_DEV):
        here = grad[i * rows : (i + 1) * rows, i * width : (i + 1) * width]
        tiles[i] = shrink_diagonal(held[i] - scale * here, quarter)
        copies[i].start()
    tiles[2] = shrink(held[2] - scale * grad[:rows, width:])

    @pl.when(slot > 0)
    def _():
        copies[2].start()

    rows_half[...] = dot_nn(p_own[quarter], s_after[...])
    for i in range(BLK_DEV):
        copies[i].wait()

    @pl.when(slot > 0)
    def _():
        copies[2].wait()


def order_halo(nat, ptq, p_cross, p_chip, quarter):
    even = is_even()
    for ref, at in ((p_cross, jnp.where(even, 0, 1)), (p_chip, jnp.where(even, 1, 0))):
        natural(nat.at[at], ref)
        ptq[at] = ref[quarter]


def update_rows(slot_of, source, grad, a_base, scale, tiles, mats):
    rows, width = grad.shape[0] // 2, grad.shape[1] // 2
    for a in range(2):
        for b in range(2):
            slot = slot_of[b * 4 + a_base + a]
            here = grad[a * rows : (a + 1) * rows, b * width : (b + 1) * width]
            tile = shrink(source[slot] - scale * here)
            tiles[a * 2 + b] = tile
            spot = (slice(a * rows, (a + 1) * rows), slice(b * width, (b + 1) * width))
            mats[spot] = jnp.where(slot > 0, tile, 0.0).astype(bf16)


def outer_kernel(
    slot_of, omega, turned, s_before, s_own, s_after, stq, cols_half, p_cross, p_chip,
    tiles, cross, chip, nat, ptq, grad, mats, half,
):
    rows, width = omega.shape[1:]
    quarter = lax.axis_index("samp")
    scale = step_size / (2.0 * s_own.shape[0])
    order_halo(nat, ptq, p_cross, p_chip, quarter)
    total = jnp.zeros(cross.shape, f32)
    for a in range(2 * BLK_DEV):
        blk = a % BLK_DEV
        at = slice(blk * width, (blk + 1) * width)
        source = (s_before, s_own)[a // BLK_DEV][:, at]
        other = dot_nt(stq[2], nat[0, at, :]) if a < BLK_DEV else cols_half[:, at]
        half[...] = dot_nn(ptq[1], source) + other
        for b in range(BLK_DEV):
            tile = shrink(turned[2 * a + b].astype(f32) - scale * half[b * rows : (b + 1) * rows, :])
            tile = jnp.where(slot_of[b * 4 + a] > 0, tile, 0.0)
            mats[b * rows : (b + 1) * rows, at] = tile.astype(bf16)
        total += dot_nt(mats[:, at], source)
    after = total.astype(bf16)
    grad[...] = dot_nn(ptq[0], s_after[...]) + dot_nt(stq[0], nat[1])
    update_rows(slot_of, omega, grad, 0, scale, tiles, mats)
    before = dot_nt(mats[...], s_after[...]).astype(bf16)
    send_halves(cross, chip, before, after)


def inner_kernel(
    slot_of, omega, s_own, s_after, stq, rows_half, p_cross, p_chip, t_own,
    tiles, own, nat, ptq, grad, mats,
):
    quarter = lax.axis_index("samp")
    scale = step_size / (2.0 * s_own.shape[0])
    order_halo(nat, ptq, p_cross, p_chip, quarter)
    grad[...] = rows_half[...] + dot_nt(stq[1], nat[1])
    update_rows(slot_of, omega, grad, BLK_DEV, scale, tiles, mats)
    own[...] = t_own[...] + dot_nt(mats[...], s_after[...])


def last_kernel(
    slot_of, outer, inner, s_after, stq, rows_half, p_cross, p_chip, begun,
    out, nat, ptq, grad, tiles, sems,
):
    rows, width = tiles.shape[1:]
    quarter = lax.axis_index("samp")
    scale = step_size / (2.0 * s_after.shape[0])
    order_halo(nat, ptq, p_cross, p_chip, quarter)
    for group in range(2):
        other = dot_nn(ptq[0], s_after[...]) if group == 0 else rows_half[...]
        grad[group] = other + dot_nt(stq[group], nat[1])
        for a in range(2):
            for b in range(2):
                unit = group * 4 + a * 2 + b
                slot = slot_of[b * 4 + group * 2 + a]
                here = grad[group, a * rows : (a + 1) * rows, b * width : (b + 1) * width]
                tiles[unit] = shrink((outer, inner)[group][a * 2 + b] - scale * here)

                @pl.when(slot > 0)
                def _(unit=unit, slot=slot):
                    pltpu.make_async_copy(tiles.at[unit], out.at[slot], sems.at[unit]).start()

    for group in range(2):
        for a in range(2):
            for b in range(2):
                unit = group * 4 + a * 2 + b
                slot = slot_of[b * 4 + group * 2 + a]

                @pl.when(slot > 0)
                def _(unit=unit, slot=slot):
                    pltpu.make_async_copy(tiles.at[unit], out.at[slot], sems.at[unit]).wait()


def shards(samples, omega, coords):
    size = lax.axis_size("tiles")
    parts = lax.axis_size("samp")
    blocks = BLK_DEV * size
    tiles, rows, width = omega.shape
    others = tiles - BLK_DEV
    count = samples.shape[0] * parts
    wide = samples.shape[1]
    both = BLK_DEV * rows
    chip = [(i, i ^ 1) for i in range(size)]
    cross = [(i, (i - 1) % size if i % 2 == 0 else (i + 1) % size) for i in range(size)]
    shape = jax.ShapeDtypeStruct
    params = pltpu.CompilerParams(vmem_limit_bytes=LIMIT)

    def call(body, in_specs, outs, scratch, macs, moved, aliases=None, out_specs=None):
        several = isinstance(outs, tuple)
        specs = out_specs or ((VMEM,) * len(outs) if several else VMEM)
        return pl.pallas_call(
            body, out_shape=outs, in_specs=in_specs, out_specs=specs, scratch_shapes=scratch,
            compiler_params=params, input_output_aliases=aliases or {},
            cost_estimate=pl.CostEstimate(flops=2 * macs, bytes_accessed=moved, transcendentals=0),
        )

    def exchange(to_cross, to_chip):
        from_chip = lax.ppermute(to_chip, "tiles", chip)
        from_cross = lax.ppermute(to_cross, "tiles", cross)
        return from_cross, from_chip

    def spread(x):
        return lax.all_to_all(jnp.broadcast_to(x[None], (parts,) + x.shape), "samp", 0, 0)

    copies, pieces = call(
        prepare_kernel, [HBM, HBM],
        (shape((parts,) + samples.shape, bf16), pltpu.HBM((parts, others, rows, rows), bf16)),
        [
            pltpu.VMEM((others, rows, width), f32), pltpu.VMEM((parts, others, rows, rows), bf16),
            pltpu.VMEM(samples.shape, bf16), pltpu.SemaphoreType.DMA,
            pltpu.SemaphoreType.DMA((others,)), pltpu.SemaphoreType.DMA((others,)),
        ],
        0, 5 << 20, out_specs=(VMEM, HBM),
    )(pltpu.with_memory_space_constraint(samples, pltpu.HBM), pltpu.with_memory_space_constraint(omega, pltpu.HBM))
    s_own = lax.all_to_all(copies, "samp", 0, 0).reshape(count, wide)
    turned_parts = lax.all_to_all(pieces, "samp", 0, 0)
    s_cross, s_chip = exchange(s_own, s_own)

    window = shape((count, wide), bf16)
    part = shape((both, count), bf16)
    full = shape((both, count), f32)
    unit = rows * width * count
    s_before, s_after, turned, to_cross, to_chip, own, slot_of = call(
        functools.partial(begin_kernel, blocks), [SMEM, VMEM, ANY, VMEM, ANY, ANY],
        (
            window, window, shape((OWN_PAIR + 1, rows, width), bf16), part, part, full,
            shape((OWN_PAIR + 1,), jnp.int32),
        ),
        [
            pltpu.VMEM((OWN_PAIR + 1, rows, width), bf16), pltpu.VMEM((parts, others, rows, rows), bf16),
            pltpu.SemaphoreType.DMA((2,)), pltpu.SemaphoreType.DMA,
        ],
        20 * unit, 6 << 20, out_specs=(VMEM,) * 6 + (SMEM,),
    )(coords, omega, turned_parts, s_own, s_cross, s_chip)

    def products(to_cross, to_chip, finish):
        from_cross, from_chip = exchange(to_cross, to_chip)
        tiles, own = finish()
        total = own + from_cross.astype(f32) + from_chip.astype(f32)
        p_own = spread(total.astype(bf16))
        p_cross, p_chip = exchange(p_own, p_own)
        return tiles, p_own, p_cross, p_chip

    grad = pltpu.VMEM((both, wide), f32)
    mats = pltpu.VMEM((both, wide), bf16)
    nat = pltpu.VMEM((2, wide, count), bf16)
    ptq = pltpu.VMEM((2, both, count), bf16)
    four = shape((4, rows, width), f32)

    _, p_own, p_cross, p_chip = products(to_cross, to_chip, lambda: (None, own))
    wide_half = shape((both, wide), f32)
    mine, t_own, _, stq, cols_half, rows_half = call(
        own_kernel, [SMEM] + [VMEM] * 6,
        (
            shape((3, rows, width), f32), full, shape((wide, count), bf16), shape((3, both, count), bf16),
            wide_half, wide_half,
        ),
        [grad, mats], 20 * unit, 6 << 20,
    )(slot_of, omega, turned, s_before, s_own, s_after, p_own)
    outer, to_cross, to_chip = call(
        outer_kernel, [SMEM] + [VMEM] * 9,
        (four, part, part), [nat, ptq, grad, mats, pltpu.VMEM((both, width), f32)], 32 * unit, 6 << 20,
    )(slot_of, omega, turned, s_before, s_own, s_after, stq, cols_half, p_cross, p_chip)

    def finish():
        return call(
            inner_kernel, [SMEM] + [VMEM] * 8,
            (four, full), [nat, ptq, grad, mats], 8 * unit, 4 << 20,
        )(slot_of, omega, s_own, s_after, stq, rows_half, p_cross, p_chip, t_own)

    inner, p_own, p_cross, p_chip = products(to_cross, to_chip, finish)
    whole = shape(omega.shape, f32)
    begun, rows_half = call(
        own_last_kernel, [SMEM] + [VMEM] * 5, (whole, wide_half),
        [grad, pltpu.VMEM((wide, count), bf16), pltpu.VMEM((3, rows, width), f32), pltpu.SemaphoreType.DMA((3,))],
        12 * unit, 3 << 20, out_specs=(ANY, VMEM),
    )(slot_of, mine, s_own, s_after, stq, p_own)
    return call(
        last_kernel, [SMEM] + [VMEM] * 7 + [ANY], whole,
        [nat, ptq, pltpu.VMEM((2, both, wide), f32), pltpu.VMEM((8, rows, width), f32), pltpu.SemaphoreType.DMA((8,))],
        12 * unit, 6 << 20, aliases={8: 0}, out_specs=ANY,
    )(slot_of, outer, inner, s_after, stq, rows_half, p_cross, p_chip, begun)


def solution(mesh):
    in_specs = (P("samp", "tiles"), P("tiles", "samp", None), P("tiles", None))
    out_specs = P("tiles", "samp", None)

    return jax.shard_map(shards, mesh=mesh, in_specs=in_specs, out_specs=out_specs, check_vma=False)
```

```python
import functools

import jax
import jax.numpy as jnp
from jax import lax
from jax.experimental import pallas as pl
from jax.experimental.pallas import tpu as pltpu
from jax.sharding import PartitionSpec as P


BLK_DEV = 2
step_size = 0.25
penalty = 0.2

VMEM = pl.BlockSpec(memory_space=pltpu.VMEM)
SMEM = pl.BlockSpec(memory_space=pltpu.SMEM)
ANY = pl.BlockSpec(memory_space=pl.ANY)
HBM = pl.BlockSpec(memory_space=pltpu.HBM)
bf16, f32 = jnp.bfloat16, jnp.float32

OWN_PAIR = 8
LIMIT = 12 << 20


def dot_nn(a, b):
    return jnp.dot(a, b, preferred_element_type=f32)


def dot_nt(a, b):
    return lax.dot_general(a, b, (((1,), (1,)), ((), ())), preferred_element_type=f32)


def shrink(value):
    level = step_size * penalty
    return value - jnp.clip(value, -level, level)


def shrink_diagonal(value, quarter):
    rows, width = value.shape
    row_ids = quarter * rows + lax.broadcasted_iota(jnp.int32, (rows, width), 0)
    col_ids = lax.broadcasted_iota(jnp.int32, (rows, width), 1)
    positive = 0.5 * (value + jnp.sqrt(value * value + 4.0 * step_size))
    return jnp.where(row_ids == col_ids, positive, shrink(value))


def find_slots(blocks, coords, slot_of):
    first = (lax.axis_index("tiles") - 1) * BLK_DEV
    for pair in range(OWN_PAIR + 1):
        slot_of[pair] = 0

    def place(slot, side):
        at = coords[slot, side] - first
        at = jnp.where(at < 0, at + blocks, at)
        return jnp.where(at >= blocks, at - blocks, at)

    for slot in range(BLK_DEV, coords.shape[0]):
        row, col = place(slot, 0), place(slot, 1)
        pair = jnp.where(col >= 2 * BLK_DEV, (col - 2 * BLK_DEV) * 2 * BLK_DEV + row, OWN_PAIR)
        slot_of[pair] = slot


def is_even():
    return lax.rem(lax.axis_index("tiles"), 2) == 0


def repeat_kernel(x, out, held, in_sem, out_sems):
    load = pltpu.make_async_copy(x, held, in_sem)
    load.start()
    load.wait()
    stores = [pltpu.make_async_copy(held, out.at[part], out_sems.at[part]) for part in range(out.shape[0])]
    for store in stores:
        store.start()
    for store in stores:
        store.wait()


def cut_kernel(omega, out, held, pieces, in_sems, out_sems):
    rows = omega.shape[1]
    others = held.shape[0]
    loads = [
        pltpu.make_async_copy(omega.at[BLK_DEV + k], held.at[k], in_sems.at[k]) for k in range(others)
    ]
    for load in loads:
        load.start()
    stores = []
    for k in range(others):
        loads[k].wait()
        for part in range(out.shape[0]):
            pieces[part, k] = held[k, :, part * rows : (part + 1) * rows].astype(bf16).T
        stores.append(pltpu.make_async_copy(pieces.at[:, k], out.at[:, k], out_sems.at[k]))
        stores[-1].start()
    for store in stores:
        store.wait()


def choose(even_is_first, first, second):
    even = is_even()

    @pl.when(even if even_is_first else jnp.logical_not(even))
    def _():
        first()

    @pl.when(jnp.logical_not(even) if even_is_first else even)
    def _():
        second()


def next_side():
    return jnp.where(is_even(), 2, 0)


def put_tile(slot, tile, mats, at):
    mats[at] = jnp.where(slot > 0, tile, 0.0).astype(bf16)


def spot(i, rows, start, width):
    return slice(i * rows, (i + 1) * rows), slice(start, start + width)


def first_rows(slot_of, omega, base, s_near, mats):
    rows, width = omega.shape[1:]
    for i in range(2):
        for blk in range(2):
            slot = slot_of[blk * 4 + base + i]
            put_tile(slot, omega[slot], mats, spot(i, rows, blk * width, width))
    return dot_nt(mats[...], s_near[...])


def first_cols(turned, s_near, s_own):
    rows, width = turned.shape[1:]
    total = jnp.zeros((2 * rows, s_own.shape[0]), f32)
    for a in range(2 * BLK_DEV):
        source = (s_near, s_own)[a // BLK_DEV]
        blk = a % BLK_DEV
        total += dot_nt(turned[2 * a : 2 * a + 2].reshape(2 * rows, width), source[:, blk * width : (blk + 1) * width])
    return total


def first_cross_kernel(blocks, coords, omega, parts, s_own, s_chip, turned, out, slot_of, mats, sems):
    rows, _ = omega.shape[1:]
    count = parts.shape[0]
    find_slots(blocks, coords, slot_of)

    def fill(pair):
        slot = slot_of[pair]
        unit = OWN_PAIR if pair == OWN_PAIR else pair % 4 * 2 + pair // 4
        copies = [
            pltpu.make_async_copy(
                parts.at[part, slot - BLK_DEV],
                turned.at[unit, :, part * rows : (part + 1) * rows],
                sems.at[pair, part],
            )
            for part in range(count)
        ]
        return slot, unit, copies

    for pair in range(OWN_PAIR + 1):
        slot, unit, copies = fill(pair)

        @pl.when(slot > 0)
        def _(copies=copies):
            for copy in copies:
                copy.start()

        @pl.when(slot == 0)
        def _(unit=unit):
            turned[unit] = jnp.zeros_like(turned[unit])

    @pl.when(is_even())
    def _():
        out[...] = first_rows(slot_of, omega, 0, s_chip, mats).astype(bf16)

    for pair in range(OWN_PAIR + 1):
        slot, unit, copies = fill(pair)

        @pl.when(slot > 0)
        def _(copies=copies):
            for copy in copies:
                copy.wait()

    @pl.when(jnp.logical_not(is_even()))
    def _():
        out[...] = first_cols(turned, s_chip, s_own).astype(bf16)


def first_chip_kernel(blocks, coords, omega, turned, s_own, s_cross, out, slot_of, mats):
    find_slots(blocks, coords, slot_of)

    def cols():
        out[...] = first_cols(turned, s_cross, s_own).astype(bf16)

    def rows():
        out[...] = first_rows(slot_of, omega, 0, s_cross, mats).astype(bf16)

    choose(True, cols, rows)


def first_own_kernel(blocks, coords, omega, turned, s_own, s_cross, s_chip, own, stq, slot_of, mats):
    rows, width = omega.shape[1:]
    quarter = lax.axis_index("samp")
    find_slots(blocks, coords, slot_of)
    mats[:rows, :width] = omega[0].astype(bf16)
    mats[rows:, width:] = omega[1].astype(bf16)
    slot = slot_of[OWN_PAIR]
    put_tile(slot, omega[slot], mats, spot(0, rows, width, width))
    mats[rows:, :width] = turned[OWN_PAIR]
    own[...] = dot_nt(mats[...], s_own[...])

    def add(s_next):
        own[...] += first_rows(slot_of, omega, BLK_DEV, s_next, mats)

    choose(True, lambda: add(s_chip), lambda: add(s_cross))
    for side, ref in enumerate((s_cross, s_own, s_chip)):
        for blk in range(BLK_DEV):
            at = pl.multiple_of(blk * width + quarter * rows, rows)
            stq[side, blk * rows : (blk + 1) * rows, :] = ref[:, pl.ds(at, rows)].T


def half_kernel(stq, p_own, out):
    count, both = p_own.shape[0], p_own.shape[1]
    rows = both // BLK_DEV
    far = stq[next_side()]
    for part in range(count):
        piece = dot_nt(far, p_own[part])
        for blk in range(BLK_DEV):
            at = (blk * count + part) * rows
            out[:, at : at + rows] = piece[:, blk * rows : (blk + 1) * rows]


def natural(out, pieces):
    count, both = pieces.shape[0], pieces.shape[1]
    rows = both // BLK_DEV
    for blk in range(BLK_DEV):
        for part in range(count):
            at = (blk * count + part) * rows
            out[at : at + rows, :] = pieces[part, blk * rows : (blk + 1) * rows, :]


def update_edge(old, slots, ptq, far, s_near, p_near, scale, grad, nat, put):
    rows, width = grad.shape[0] // 2, grad.shape[1] // 2
    natural(nat, p_near)
    grad[...] = dot_nn(ptq, s_near[...]) + dot_nt(far, nat[...])
    for i in range(2):
        for blk in range(2):
            slot = slots(i, blk)
            put(i, blk, slot, shrink(old(i, blk, slot) - scale * grad[spot(i, rows, blk * width, width)]))


def edge_kernel(
    blocks, far_side, coords, omega, turned, s_own, s_near, p_near, p_far, stq, own_half,
    tiles, out, slot_of, grad, mats, nat,
):
    rows, width = omega.shape[1:]
    wide = s_own.shape[1]
    quarter = lax.axis_index("samp")
    scale = step_size / (2.0 * s_own.shape[0])
    find_slots(blocks, coords, slot_of)

    def far_rows():
        return p_far[quarter] if far_side else p_far[...]

    def row_tiles():
        def put(i, blk, slot, tile):
            tiles[i * 2 + blk] = tile
            put_tile(slot, tile, mats, spot(i, rows, blk * width, width))

        update_edge(
            lambda i, blk, slot: omega[slot], lambda i, blk: slot_of[blk * 4 + i],
            far_rows(), stq[far_side], s_near, p_near, scale, grad, nat, put,
        )
        out[...] = dot_nt(mats[:, :wide], s_near[...]).astype(bf16)

    def col_tiles():
        def put(i, blk, slot, tile):
            put_tile(slot, tile, mats, spot(i, rows, blk * width, width))

        update_edge(
            lambda i, blk, slot: turned[2 * blk + i].astype(f32),
            lambda i, blk: slot_of[i * 4 + blk],
            far_rows(), stq[far_side], s_near, p_near, scale, grad, nat, put,
        )
        grad[...] = dot_nn(far_rows(), s_own[...]) + own_half[...]
        for i in range(2):
            for blk in range(2):
                tile = turned[2 * (BLK_DEV + blk) + i].astype(f32) - scale * grad[spot(i, rows, blk * width, width)]
                put_tile(slot_of[i * 4 + BLK_DEV + blk], shrink(tile), mats, spot(i, rows, wide + blk * width, width))
        total = dot_nt(mats[:, :wide], s_near[...]) + dot_nt(mats[:, wide:], s_own[...])
        out[...] = total.astype(bf16)

    choose(far_side == 0, row_tiles, col_tiles)


def own_kernel(blocks, coords, omega, turned, s_own, stq, p_own, tiles, t_own, slot_of, grad, mats, nat_own):
    rows, width = grad.shape[0] // 2, grad.shape[1] // 2
    quarter = lax.axis_index("samp")
    scale = step_size / (2.0 * s_own.shape[0])
    find_slots(blocks, coords, slot_of)
    natural(nat_own, p_own)
    grad[...] = dot_nn(p_own[quarter], s_own[...]) + dot_nt(stq[1], nat_own[...])
    slot = slot_of[OWN_PAIR]
    for i in range(BLK_DEV):
        here = grad[spot(i, rows, i * width, width)]
        tiles[i] = shrink_diagonal(omega[i] - scale * here, quarter)
        mats[spot(i, rows, i * width, width)] = tiles[i].astype(bf16)
    tiles[2] = shrink(omega[slot] - scale * grad[:rows, width:])
    put_tile(slot, tiles[2], mats, spot(0, rows, width, width))
    there = turned[OWN_PAIR].astype(f32) - scale * grad[rows:, :width]
    put_tile(slot, shrink(there), mats, spot(1, rows, 0, width))
    t_own[...] = dot_nt(mats[...], s_own[...])


def inner_kernel(
    blocks, coords, omega, s_cross, s_chip, stq, p_own, p_cross, p_chip, t_own, tiles, own, slot_of, grad, mats, nat
):
    rows, width = omega.shape[1:]
    quarter = lax.axis_index("samp")
    scale = step_size / (2.0 * s_chip.shape[0])
    find_slots(blocks, coords, slot_of)

    def put(i, blk, slot, tile):
        tiles[i * 2 + blk] = tile
        put_tile(slot, tile, mats, spot(i, rows, blk * width, width))

    def run(s_next, p_next):
        update_edge(
            lambda i, blk, slot: omega[slot],
            lambda i, blk: slot_of[blk * 4 + BLK_DEV + i],
            p_own[quarter], stq[1], s_next, p_next, scale, grad, nat, put,
        )
        own[...] = t_own[...] + dot_nt(mats[...], s_next[...])

    choose(True, lambda: run(s_chip, p_chip), lambda: run(s_cross, p_cross))


def own_last_kernel(
    blocks, coords, held, s_own, s_cross, s_chip, stq, p_own, out, rows_half, slot_of, grad, nat_own, tiles, sems,
):
    rows, width = grad.shape[0] // 2, grad.shape[1] // 2
    quarter = lax.axis_index("samp")
    scale = step_size / (2.0 * s_own.shape[0])
    find_slots(blocks, coords, slot_of)
    natural(nat_own, p_own)
    grad[...] = dot_nn(p_own[quarter], s_own[...]) + dot_nt(stq[1], nat_own[...])
    slot = slot_of[OWN_PAIR]
    copies = [pltpu.make_async_copy(tiles.at[i], out.at[i], sems.at[i]) for i in range(BLK_DEV)]
    copies.append(pltpu.make_async_copy(tiles.at[2], out.at[slot], sems.at[2]))
    for i in range(BLK_DEV):
        here = grad[i * rows : (i + 1) * rows, i * width : (i + 1) * width]
        tiles[i] = shrink_diagonal(held[i] - scale * here, quarter)
        copies[i].start()
    tiles[2] = shrink(held[2] - scale * grad[:rows, width:])

    @pl.when(slot > 0)
    def _():
        copies[2].start()

    def half(s_next):
        rows_half[...] = dot_nn(p_own[quarter], s_next[...])

    choose(True, lambda: half(s_chip), lambda: half(s_cross))
    for i in range(BLK_DEV):
        copies[i].wait()

    @pl.when(slot > 0)
    def _():
        copies[2].wait()


def last_kernel(
    blocks, coords, outer_cross, outer_chip, inner, s_cross, s_chip, stq, rows_half, p_cross, p_chip, begun,
    out, slot_of, grad, nat, tiles, sems,
):
    rows, width = tiles.shape[1:]
    quarter = lax.axis_index("samp")
    scale = step_size / (2.0 * s_chip.shape[0])
    find_slots(blocks, coords, slot_of)

    def copy(unit, slot):
        return pltpu.make_async_copy(tiles.at[unit], out.at[slot], sems.at[unit])

    def slot_at(group, i, blk):
        return slot_of[blk * 4 + group * BLK_DEV + i]

    def run(outer, s_next, p_next, p_far, far):
        natural(nat, p_next)
        for group in (1, 0):
            other = rows_half[...] if group else dot_nn(p_far[quarter], s_next[...])
            grad[group] = other + dot_nt((far, stq[1])[group], nat[...])
            for i in range(2):
                for blk in range(2):
                    here = grad[(group,) + spot(i, rows, blk * width, width)]
                    unit, slot = group * 4 + i * 2 + blk, slot_at(group, i, blk)
                    tiles[unit] = shrink((outer, inner)[group][i * 2 + blk] - scale * here)

                    @pl.when(slot > 0)
                    def _(unit=unit, slot=slot):
                        copy(unit, slot).start()

    choose(
        True,
        lambda: run(outer_cross, s_chip, p_chip, p_cross, stq[0]),
        lambda: run(outer_chip, s_cross, p_cross, p_chip, stq[2]),
    )
    for group in range(2):
        for i in range(2):
            for blk in range(2):
                unit, slot = group * 4 + i * 2 + blk, slot_at(group, i, blk)

                @pl.when(slot > 0)
                def _(unit=unit, slot=slot):
                    copy(unit, slot).wait()


def shards(samples, omega, coords):
    size = lax.axis_size("tiles")
    parts = lax.axis_size("samp")
    blocks = BLK_DEV * size
    tiles, rows, width = omega.shape
    others = tiles - BLK_DEV
    count = samples.shape[0] * parts
    wide = samples.shape[1]
    both = BLK_DEV * rows
    chip = [(i, i ^ 1) for i in range(size)]
    cross = [(i, (i - 1) % size if i % 2 == 0 else (i + 1) % size) for i in range(size)]
    shape = jax.ShapeDtypeStruct
    slots = pltpu.SMEM((OWN_PAIR + 1,), jnp.int32)
    params = pltpu.CompilerParams(vmem_limit_bytes=LIMIT)

    def call(body, in_specs, outs, scratch, macs, moved, aliases=None, out_specs=None):
        several = isinstance(outs, tuple)
        specs = out_specs or ((VMEM,) * len(outs) if several else VMEM)
        return pl.pallas_call(
            body, out_shape=outs, in_specs=in_specs, out_specs=specs, scratch_shapes=scratch,
            compiler_params=params, input_output_aliases=aliases or {},
            cost_estimate=pl.CostEstimate(flops=2 * macs, bytes_accessed=moved, transcendentals=0),
        )

    def permute(x, pairs):
        return lax.ppermute(x, "tiles", pairs)

    def spread(x):
        return lax.all_to_all(jnp.broadcast_to(x[None], (parts,) + x.shape), "samp", 0, 0)

    copies = call(
        repeat_kernel, [HBM], pltpu.HBM((parts,) + samples.shape, bf16),
        [pltpu.VMEM(samples.shape, bf16), pltpu.SemaphoreType.DMA, pltpu.SemaphoreType.DMA((parts,))],
        0, 1 << 20, out_specs=HBM,
    )(pltpu.with_memory_space_constraint(samples, pltpu.HBM))
    s_own = lax.all_to_all(copies, "samp", 0, 0).reshape(count, wide)
    pieces = call(
        cut_kernel, [HBM], pltpu.HBM((parts, others, rows, rows), bf16),
        [
            pltpu.VMEM((others, rows, width), f32), pltpu.VMEM((parts, others, rows, rows), bf16),
            pltpu.SemaphoreType.DMA((others,)), pltpu.SemaphoreType.DMA((others,)),
        ],
        0, 4 << 20, out_specs=HBM,
    )(pltpu.with_memory_space_constraint(omega, pltpu.HBM))
    turned_parts = lax.all_to_all(pieces, "samp", 0, 0)
    s_cross = permute(s_own, cross)
    s_chip = permute(s_own, chip)

    part = shape((both, count), bf16)
    full = shape((both, count), f32)
    four = shape((4, rows, width), f32)
    wide_half = shape((both, wide), f32)
    unit = rows * width * count
    grad = pltpu.VMEM((both, wide), f32)
    mats = pltpu.VMEM((both, wide), bf16)
    mats_two = pltpu.VMEM((both, 2 * wide), bf16)
    nat = pltpu.VMEM((wide, count), bf16)

    def run(body, args, in_specs, outs, scratch, units, out_specs=None, aliases=None):
        return call(body, in_specs, outs, scratch, units * unit, 4 << 20, aliases, out_specs)(*args)

    def kernel(body, *extra):
        return functools.partial(body, blocks, *extra)

    turned, to_cross = run(
        kernel(first_cross_kernel), (coords, omega, turned_parts, s_own, s_chip), [SMEM, VMEM, ANY, VMEM, VMEM],
        (shape((OWN_PAIR + 1, rows, width), bf16), part),
        [slots, mats, pltpu.SemaphoreType.DMA((OWN_PAIR + 1, parts))], 8,
    )
    from_cross = permute(to_cross, cross)
    to_chip = run(
        kernel(first_chip_kernel), (coords, omega, turned, s_own, s_cross), [SMEM] + [VMEM] * 4,
        part, [slots, mats], 8,
    )
    from_chip = permute(to_chip, chip)
    own, stq = run(
        kernel(first_own_kernel), (coords, omega, turned, s_own, s_cross, s_chip), [SMEM] + [VMEM] * 5,
        (full, shape((3, both, count), bf16)), [slots, mats], 8,
    )
    total = (own + from_cross.astype(f32) + from_chip.astype(f32)).astype(bf16)
    far_cross = permute(total, cross)
    p_own = spread(total)
    p_cross = permute(p_own, cross)
    p_chip = permute(p_own, chip)
    own_half = run(half_kernel, (stq, p_own), [VMEM] * 2, wide_half, [], 4)

    def edge(side, s_near, p_near, p_far):
        return run(
            kernel(edge_kernel, side), (coords, omega, turned, s_own, s_near, p_near, p_far, stq, own_half),
            [SMEM] + [VMEM] * 8, (four, part), [slots, grad, mats_two, nat], 20,
        )

    outer_cross, to_cross = edge(0, s_chip, p_chip, far_cross)
    from_cross = permute(to_cross, cross)
    mine, t_own = run(
        kernel(own_kernel), (coords, omega, turned, s_own, stq, p_own), [SMEM] + [VMEM] * 5,
        (shape((3, rows, width), f32), full), [slots, grad, mats, nat], 12,
    )
    outer_chip, to_chip = edge(2, s_cross, p_cross, p_chip)
    from_chip = permute(to_chip, chip)
    inner, own = run(
        kernel(inner_kernel), (coords, omega, s_cross, s_chip, stq, p_own, p_cross, p_chip, t_own),
        [SMEM] + [VMEM] * 8, (four, full), [slots, grad, mats, nat], 12,
    )
    total = (own + from_cross.astype(f32) + from_chip.astype(f32)).astype(bf16)
    p_own = spread(total)
    p_cross = permute(p_own, cross)
    p_chip = permute(p_own, chip)
    whole = shape(omega.shape, f32)
    begun, rows_half = run(
        kernel(own_last_kernel), (coords, mine, s_own, s_cross, s_chip, stq, p_own), [SMEM] + [VMEM] * 6,
        (whole, wide_half),
        [slots, grad, nat, pltpu.VMEM((3, rows, width), f32), pltpu.SemaphoreType.DMA((3,))],
        12, out_specs=(ANY, VMEM),
    )
    return run(
        kernel(last_kernel),
        (coords, outer_cross, outer_chip, inner, s_cross, s_chip, stq, rows_half, p_cross, p_chip, begun),
        [SMEM] + [VMEM] * 9 + [ANY], whole,
        [slots, pltpu.VMEM((2, both, wide), f32), nat, pltpu.VMEM((8, rows, width), f32), pltpu.SemaphoreType.DMA((8,))],
        12, out_specs=ANY, aliases={10: 0},
    )


def solution(mesh):
    in_specs = (P("samp", "tiles"), P("tiles", "samp", None), P("tiles", None))
    out_specs = P("tiles", "samp", None)

    return jax.shard_map(shards, mesh=mesh, in_specs=in_specs, out_specs=out_specs, check_vma=False)
```

```python
import functools

import jax
import jax.numpy as jnp
from jax import lax
from jax.experimental import pallas as pl
from jax.experimental.pallas import tpu as pltpu
from jax.sharding import PartitionSpec as P


BLK_DEV = 2
step_size = 0.25
penalty = 0.2

VMEM = pl.BlockSpec(memory_space=pltpu.VMEM)
SMEM = pl.BlockSpec(memory_space=pltpu.SMEM)
ANY = pl.BlockSpec(memory_space=pl.ANY)
HBM = pl.BlockSpec(memory_space=pltpu.HBM)
bf16, f32 = jnp.bfloat16, jnp.float32

OWN_PAIR = 8
LIMIT = 12 << 20


def dot_nn(a, b):
    return jnp.dot(a, b, preferred_element_type=f32)


def dot_nt(a, b):
    return lax.dot_general(a, b, (((1,), (1,)), ((), ())), preferred_element_type=f32)


def shrink(value):
    level = step_size * penalty
    return value - jnp.clip(value, -level, level)


def shrink_diagonal(value, quarter):
    rows, width = value.shape
    row_ids = quarter * rows + lax.broadcasted_iota(jnp.int32, (rows, width), 0)
    col_ids = lax.broadcasted_iota(jnp.int32, (rows, width), 1)
    positive = 0.5 * (value + jnp.sqrt(value * value + 4.0 * step_size))
    return jnp.where(row_ids == col_ids, positive, shrink(value))


def find_slots(blocks, coords, slot_of):
    first = (lax.axis_index("tiles") - 1) * BLK_DEV
    for pair in range(OWN_PAIR + 1):
        slot_of[pair] = 0

    def place(slot, side):
        at = coords[slot, side] - first
        at = jnp.where(at < 0, at + blocks, at)
        return jnp.where(at >= blocks, at - blocks, at)

    for slot in range(BLK_DEV, coords.shape[0]):
        row, col = place(slot, 0), place(slot, 1)
        pair = jnp.where(col >= 2 * BLK_DEV, (col - 2 * BLK_DEV) * 2 * BLK_DEV + row, OWN_PAIR)
        slot_of[pair] = slot


def is_even():
    return lax.rem(lax.axis_index("tiles"), 2) == 0


def repeat_kernel(x, out, held, in_sem, out_sems):
    load = pltpu.make_async_copy(x, held, in_sem)
    load.start()
    load.wait()
    stores = [pltpu.make_async_copy(held, out.at[part], out_sems.at[part]) for part in range(out.shape[0])]
    for store in stores:
        store.start()
    for store in stores:
        store.wait()


def cut_kernel(omega, out, held, pieces, in_sems, out_sems):
    rows = omega.shape[1]
    others = held.shape[0]
    loads = [
        pltpu.make_async_copy(omega.at[BLK_DEV + k], held.at[k], in_sems.at[k]) for k in range(others)
    ]
    for load in loads:
        load.start()
    stores = []
    for k in range(others):
        loads[k].wait()
        for part in range(out.shape[0]):
            pieces[part, k] = held[k, :, part * rows : (part + 1) * rows].astype(bf16).T
        stores.append(pltpu.make_async_copy(pieces.at[:, k], out.at[:, k], out_sems.at[k]))
        stores[-1].start()
    for store in stores:
        store.wait()


def choose(even_is_first, first, second):
    even = is_even()

    @pl.when(even if even_is_first else jnp.logical_not(even))
    def _():
        first()

    @pl.when(jnp.logical_not(even) if even_is_first else even)
    def _():
        second()


def next_side():
    return jnp.where(is_even(), 2, 0)


def put_tile(slot, tile, mats, at):
    mats[at] = jnp.where(slot > 0, tile, 0.0).astype(bf16)


def spot(i, rows, start, width):
    return slice(i * rows, (i + 1) * rows), slice(start, start + width)


def first_rows(slot_of, omega, base, s_near, mats):
    rows, width = omega.shape[1:]
    for i in range(2):
        for blk in range(2):
            slot = slot_of[blk * 4 + base + i]
            put_tile(slot, omega[slot], mats, spot(i, rows, blk * width, width))
    return dot_nt(mats[...], s_near[...])


def first_cols(turned, s_near, s_own):
    rows, width = turned.shape[1:]
    total = jnp.zeros((2 * rows, s_own.shape[0]), f32)
    for a in range(2 * BLK_DEV):
        source = (s_near, s_own)[a // BLK_DEV]
        blk = a % BLK_DEV
        total += dot_nt(turned[2 * a : 2 * a + 2].reshape(2 * rows, width), source[:, blk * width : (blk + 1) * width])
    return total


def first_cross_kernel(blocks, coords, omega, parts, s_own, s_in, turned, out, s_chip, slot_of, mats, sems, s_sem):
    window = pltpu.make_async_copy(s_in, s_chip, s_sem)
    window.start()
    rows, _ = omega.shape[1:]
    count = parts.shape[0]
    find_slots(blocks, coords, slot_of)

    def fill(pair):
        slot = slot_of[pair]
        unit = OWN_PAIR if pair == OWN_PAIR else pair % 4 * 2 + pair // 4
        copies = [
            pltpu.make_async_copy(
                parts.at[part, slot - BLK_DEV],
                turned.at[unit, :, part * rows : (part + 1) * rows],
                sems.at[pair, part],
            )
            for part in range(count)
        ]
        return slot, unit, copies

    for pair in range(OWN_PAIR + 1):
        slot, unit, copies = fill(pair)

        @pl.when(slot > 0)
        def _(copies=copies):
            for copy in copies:
                copy.start()

        @pl.when(slot == 0)
        def _(unit=unit):
            turned[unit] = jnp.zeros_like(turned[unit])

    window.wait()

    @pl.when(is_even())
    def _():
        out[...] = first_rows(slot_of, omega, 0, s_chip, mats).astype(bf16)

    for pair in range(OWN_PAIR + 1):
        slot, unit, copies = fill(pair)

        @pl.when(slot > 0)
        def _(copies=copies):
            for copy in copies:
                copy.wait()

    @pl.when(jnp.logical_not(is_even()))
    def _():
        out[...] = first_cols(turned, s_chip, s_own).astype(bf16)


def first_chip_kernel(blocks, coords, omega, turned, s_own, s_in, out, s_cross, slot_of, mats, s_sem):
    window = pltpu.make_async_copy(s_in, s_cross, s_sem)
    window.start()
    find_slots(blocks, coords, slot_of)
    window.wait()

    def cols():
        out[...] = first_cols(turned, s_cross, s_own).astype(bf16)

    def rows():
        out[...] = first_rows(slot_of, omega, 0, s_cross, mats).astype(bf16)

    choose(True, cols, rows)


def first_own_kernel(blocks, coords, omega, turned, s_own, s_cross, s_chip, own, stq, slot_of, mats):
    rows, width = omega.shape[1:]
    quarter = lax.axis_index("samp")
    find_slots(blocks, coords, slot_of)
    mats[:rows, :width] = omega[0].astype(bf16)
    mats[rows:, width:] = omega[1].astype(bf16)
    slot = slot_of[OWN_PAIR]
    put_tile(slot, omega[slot], mats, spot(0, rows, width, width))
    mats[rows:, :width] = turned[OWN_PAIR]
    own[...] = dot_nt(mats[...], s_own[...])

    def add(s_next):
        own[...] += first_rows(slot_of, omega, BLK_DEV, s_next, mats)

    choose(True, lambda: add(s_chip), lambda: add(s_cross))
    for side, ref in enumerate((s_cross, s_own, s_chip)):
        for blk in range(BLK_DEV):
            at = pl.multiple_of(blk * width + quarter * rows, rows)
            stq[side, blk * rows : (blk + 1) * rows, :] = ref[:, pl.ds(at, rows)].T


def half_kernel(stq, p_own, out):
    count, both = p_own.shape[0], p_own.shape[1]
    rows = both // BLK_DEV
    far = stq[next_side()]
    for part in range(count):
        piece = dot_nt(far, p_own[part])
        for blk in range(BLK_DEV):
            at = (blk * count + part) * rows
            out[:, at : at + rows] = piece[:, blk * rows : (blk + 1) * rows]


def natural(out, pieces):
    count, both = pieces.shape[0], pieces.shape[1]
    rows = both // BLK_DEV
    for blk in range(BLK_DEV):
        for part in range(count):
            at = (blk * count + part) * rows
            out[at : at + rows, :] = pieces[part, blk * rows : (blk + 1) * rows, :]


def update_edge(old, slots, ptq, far, s_near, p_near, scale, grad, nat, put):
    rows, width = grad.shape[0] // 2, grad.shape[1] // 2
    natural(nat, p_near)
    grad[...] = dot_nn(ptq, s_near[...]) + dot_nt(far, nat[...])
    for i in range(2):
        for blk in range(2):
            slot = slots(i, blk)
            put(i, blk, slot, shrink(old(i, blk, slot) - scale * grad[spot(i, rows, blk * width, width)]))


def edge_kernel(
    blocks, far_side, coords, omega, turned, s_own, s_near, p_near, p_far, stq, own_half,
    tiles, out, slot_of, grad, mats, nat,
):
    rows, width = omega.shape[1:]
    wide = s_own.shape[1]
    quarter = lax.axis_index("samp")
    scale = step_size / (2.0 * s_own.shape[0])
    find_slots(blocks, coords, slot_of)

    def far_rows():
        return p_far[quarter] if far_side else p_far[...]

    def row_tiles():
        def put(i, blk, slot, tile):
            tiles[i * 2 + blk] = tile
            put_tile(slot, tile, mats, spot(i, rows, blk * width, width))

        update_edge(
            lambda i, blk, slot: omega[slot], lambda i, blk: slot_of[blk * 4 + i],
            far_rows(), stq[far_side], s_near, p_near, scale, grad, nat, put,
        )
        out[...] = dot_nt(mats[:, :wide], s_near[...]).astype(bf16)

    def col_tiles():
        def put(i, blk, slot, tile):
            put_tile(slot, tile, mats, spot(i, rows, blk * width, width))

        update_edge(
            lambda i, blk, slot: turned[2 * blk + i].astype(f32),
            lambda i, blk: slot_of[i * 4 + blk],
            far_rows(), stq[far_side], s_near, p_near, scale, grad, nat, put,
        )
        grad[...] = dot_nn(far_rows(), s_own[...]) + own_half[...]
        for i in range(2):
            for blk in range(2):
                tile = turned[2 * (BLK_DEV + blk) + i].astype(f32) - scale * grad[spot(i, rows, blk * width, width)]
                put_tile(slot_of[i * 4 + BLK_DEV + blk], shrink(tile), mats, spot(i, rows, wide + blk * width, width))
        total = dot_nt(mats[:, :wide], s_near[...]) + dot_nt(mats[:, wide:], s_own[...])
        out[...] = total.astype(bf16)

    choose(far_side == 0, row_tiles, col_tiles)


def own_kernel(blocks, coords, omega, turned, s_own, stq, p_own, tiles, t_own, slot_of, grad, mats, nat_own):
    rows, width = grad.shape[0] // 2, grad.shape[1] // 2
    quarter = lax.axis_index("samp")
    scale = step_size / (2.0 * s_own.shape[0])
    find_slots(blocks, coords, slot_of)
    natural(nat_own, p_own)
    grad[...] = dot_nn(p_own[quarter], s_own[...]) + dot_nt(stq[1], nat_own[...])
    slot = slot_of[OWN_PAIR]
    for i in range(BLK_DEV):
        here = grad[spot(i, rows, i * width, width)]
        tiles[i] = shrink_diagonal(omega[i] - scale * here, quarter)
        mats[spot(i, rows, i * width, width)] = tiles[i].astype(bf16)
    tiles[2] = shrink(omega[slot] - scale * grad[:rows, width:])
    put_tile(slot, tiles[2], mats, spot(0, rows, width, width))
    there = turned[OWN_PAIR].astype(f32) - scale * grad[rows:, :width]
    put_tile(slot, shrink(there), mats, spot(1, rows, 0, width))
    t_own[...] = dot_nt(mats[...], s_own[...])


def inner_kernel(
    blocks, coords, omega, s_cross, s_chip, stq, p_own, p_cross, p_chip, t_own, tiles, own, slot_of, grad, mats, nat
):
    rows, width = omega.shape[1:]
    quarter = lax.axis_index("samp")
    scale = step_size / (2.0 * s_chip.shape[0])
    find_slots(blocks, coords, slot_of)

    def put(i, blk, slot, tile):
        tiles[i * 2 + blk] = tile
        put_tile(slot, tile, mats, spot(i, rows, blk * width, width))

    def run(s_next, p_next):
        update_edge(
            lambda i, blk, slot: omega[slot],
            lambda i, blk: slot_of[blk * 4 + BLK_DEV + i],
            p_own[quarter], stq[1], s_next, p_next, scale, grad, nat, put,
        )
        own[...] = t_own[...] + dot_nt(mats[...], s_next[...])

    choose(True, lambda: run(s_chip, p_chip), lambda: run(s_cross, p_cross))


def own_last_kernel(
    blocks, coords, held, s_own, s_cross, s_chip, stq, p_own, out, rows_half, slot_of, grad, nat_own, tiles, sems,
):
    rows, width = grad.shape[0] // 2, grad.shape[1] // 2
    quarter = lax.axis_index("samp")
    scale = step_size / (2.0 * s_own.shape[0])
    find_slots(blocks, coords, slot_of)
    natural(nat_own, p_own)
    grad[...] = dot_nn(p_own[quarter], s_own[...]) + dot_nt(stq[1], nat_own[...])
    slot = slot_of[OWN_PAIR]
    copies = [pltpu.make_async_copy(tiles.at[i], out.at[i], sems.at[i]) for i in range(BLK_DEV)]
    copies.append(pltpu.make_async_copy(tiles.at[2], out.at[slot], sems.at[2]))
    for i in range(BLK_DEV):
        here = grad[i * rows : (i + 1) * rows, i * width : (i + 1) * width]
        tiles[i] = shrink_diagonal(held[i] - scale * here, quarter)
        copies[i].start()
    tiles[2] = shrink(held[2] - scale * grad[:rows, width:])

    @pl.when(slot > 0)
    def _():
        copies[2].start()

    def half(s_next):
        rows_half[...] = dot_nn(p_own[quarter], s_next[...])

    choose(True, lambda: half(s_chip), lambda: half(s_cross))
    for i in range(BLK_DEV):
        copies[i].wait()

    @pl.when(slot > 0)
    def _():
        copies[2].wait()


def last_kernel(
    blocks, coords, outer_cross, outer_chip, inner, s_cross, s_chip, stq, rows_half, p_cross, p_chip, begun,
    out, slot_of, grad, nat, tiles, sems,
):
    rows, width = tiles.shape[1:]
    quarter = lax.axis_index("samp")
    scale = step_size / (2.0 * s_chip.shape[0])
    find_slots(blocks, coords, slot_of)

    def copy(unit, slot):
        return pltpu.make_async_copy(tiles.at[unit], out.at[slot], sems.at[unit])

    def slot_at(group, i, blk):
        return slot_of[blk * 4 + group * BLK_DEV + i]

    def run(outer, s_next, p_next, p_far, far):
        natural(nat, p_next)
        for group in (1, 0):
            other = rows_half[...] if group else dot_nn(p_far[quarter], s_next[...])
            grad[group] = other + dot_nt((far, stq[1])[group], nat[...])
            for i in range(2):
                for blk in range(2):
                    here = grad[(group,) + spot(i, rows, blk * width, width)]
                    unit, slot = group * 4 + i * 2 + blk, slot_at(group, i, blk)
                    tiles[unit] = shrink((outer, inner)[group][i * 2 + blk] - scale * here)

                    @pl.when(slot > 0)
                    def _(unit=unit, slot=slot):
                        copy(unit, slot).start()

    choose(
        True,
        lambda: run(outer_cross, s_chip, p_chip, p_cross, stq[0]),
        lambda: run(outer_chip, s_cross, p_cross, p_chip, stq[2]),
    )
    for group in range(2):
        for i in range(2):
            for blk in range(2):
                unit, slot = group * 4 + i * 2 + blk, slot_at(group, i, blk)

                @pl.when(slot > 0)
                def _(unit=unit, slot=slot):
                    copy(unit, slot).wait()


def shards(samples, omega, coords):
    size = lax.axis_size("tiles")
    parts = lax.axis_size("samp")
    blocks = BLK_DEV * size
    tiles, rows, width = omega.shape
    others = tiles - BLK_DEV
    count = samples.shape[0] * parts
    wide = samples.shape[1]
    both = BLK_DEV * rows
    chip = [(i, i ^ 1) for i in range(size)]
    cross = [(i, (i - 1) % size if i % 2 == 0 else (i + 1) % size) for i in range(size)]
    shape = jax.ShapeDtypeStruct
    slots = pltpu.SMEM((OWN_PAIR + 1,), jnp.int32)
    params = pltpu.CompilerParams(vmem_limit_bytes=LIMIT)

    def call(body, in_specs, outs, scratch, macs, moved, aliases=None, out_specs=None):
        several = isinstance(outs, tuple)
        specs = out_specs or ((VMEM,) * len(outs) if several else VMEM)
        return pl.pallas_call(
            body, out_shape=outs, in_specs=in_specs, out_specs=specs, scratch_shapes=scratch,
            compiler_params=params, input_output_aliases=aliases or {},
            cost_estimate=pl.CostEstimate(flops=2 * macs, bytes_accessed=moved, transcendentals=0),
        )

    def permute(x, pairs):
        return lax.ppermute(x, "tiles", pairs)

    def spread(x):
        return lax.all_to_all(jnp.broadcast_to(x[None], (parts,) + x.shape), "samp", 0, 0)

    copies = call(
        repeat_kernel, [HBM], pltpu.HBM((parts,) + samples.shape, bf16),
        [pltpu.VMEM(samples.shape, bf16), pltpu.SemaphoreType.DMA, pltpu.SemaphoreType.DMA((parts,))],
        0, 1 << 20, out_specs=HBM,
    )(pltpu.with_memory_space_constraint(samples, pltpu.HBM))
    s_own = lax.all_to_all(copies, "samp", 0, 0).reshape(count, wide)
    pieces = call(
        cut_kernel, [HBM], pltpu.HBM((parts, others, rows, rows), bf16),
        [
            pltpu.VMEM((others, rows, width), f32), pltpu.VMEM((parts, others, rows, rows), bf16),
            pltpu.SemaphoreType.DMA((others,)), pltpu.SemaphoreType.DMA((others,)),
        ],
        0, 4 << 20, out_specs=HBM,
    )(pltpu.with_memory_space_constraint(omega, pltpu.HBM))
    turned_parts = lax.all_to_all(pieces, "samp", 0, 0)
    s_cross = permute(s_own, cross)
    s_chip = permute(s_own, chip)

    part = shape((both, count), bf16)
    full = shape((both, count), f32)
    four = shape((4, rows, width), f32)
    wide_half = shape((both, wide), f32)
    unit = rows * width * count
    grad = pltpu.VMEM((both, wide), f32)
    mats = pltpu.VMEM((both, wide), bf16)
    mats_two = pltpu.VMEM((both, 2 * wide), bf16)
    nat = pltpu.VMEM((wide, count), bf16)

    def run(body, args, in_specs, outs, scratch, units, out_specs=None, aliases=None):
        return call(body, in_specs, outs, scratch, units * unit, 4 << 20, aliases, out_specs)(*args)

    def kernel(body, *extra):
        return functools.partial(body, blocks, *extra)

    turned, to_cross, s_chip = run(
        kernel(first_cross_kernel), (coords, omega, turned_parts, s_own, s_chip), [SMEM, VMEM, ANY, VMEM, ANY],
        (shape((OWN_PAIR + 1, rows, width), bf16), part, shape((count, wide), bf16)),
        [slots, mats, pltpu.SemaphoreType.DMA((OWN_PAIR + 1, parts)), pltpu.SemaphoreType.DMA], 8,
    )
    from_cross = permute(to_cross, cross)
    to_chip, s_cross = run(
        kernel(first_chip_kernel), (coords, omega, turned, s_own, s_cross), [SMEM] + [VMEM] * 3 + [ANY],
        (part, shape((count, wide), bf16)), [slots, mats, pltpu.SemaphoreType.DMA], 8,
    )
    from_chip = permute(to_chip, chip)
    own, stq = run(
        kernel(first_own_kernel), (coords, omega, turned, s_own, s_cross, s_chip), [SMEM] + [VMEM] * 5,
        (full, shape((3, both, count), bf16)), [slots, mats], 8,
    )
    total = (own + from_cross.astype(f32) + from_chip.astype(f32)).astype(bf16)
    far_cross = permute(total, cross)
    p_own = spread(total)
    p_cross = permute(p_own, cross)
    p_chip = permute(p_own, chip)
    own_half = run(half_kernel, (stq, p_own), [VMEM] * 2, wide_half, [], 4)

    def edge(side, s_near, p_near, p_far):
        return run(
            kernel(edge_kernel, side), (coords, omega, turned, s_own, s_near, p_near, p_far, stq, own_half),
            [SMEM] + [VMEM] * 8, (four, part), [slots, grad, mats_two, nat], 20,
        )

    outer_cross, to_cross = edge(0, s_chip, p_chip, far_cross)
    from_cross = permute(to_cross, cross)
    mine, t_own = run(
        kernel(own_kernel), (coords, omega, turned, s_own, stq, p_own), [SMEM] + [VMEM] * 5,
        (shape((3, rows, width), f32), full), [slots, grad, mats, nat], 12,
    )
    outer_chip, to_chip = edge(2, s_cross, p_cross, p_chip)
    from_chip = permute(to_chip, chip)
    inner, own = run(
        kernel(inner_kernel), (coords, omega, s_cross, s_chip, stq, p_own, p_cross, p_chip, t_own),
        [SMEM] + [VMEM] * 8, (four, full), [slots, grad, mats, nat], 12,
    )
    total = (own + from_cross.astype(f32) + from_chip.astype(f32)).astype(bf16)
    p_own = spread(total)
    p_cross = permute(p_own, cross)
    p_chip = permute(p_own, chip)
    whole = shape(omega.shape, f32)
    begun, rows_half = run(
        kernel(own_last_kernel), (coords, mine, s_own, s_cross, s_chip, stq, p_own), [SMEM] + [VMEM] * 6,
        (whole, wide_half),
        [slots, grad, nat, pltpu.VMEM((3, rows, width), f32), pltpu.SemaphoreType.DMA((3,))],
        12, out_specs=(ANY, VMEM),
    )
    return run(
        kernel(last_kernel),
        (coords, outer_cross, outer_chip, inner, s_cross, s_chip, stq, rows_half, p_cross, p_chip, begun),
        [SMEM] + [VMEM] * 9 + [ANY], whole,
        [slots, pltpu.VMEM((2, both, wide), f32), nat, pltpu.VMEM((8, rows, width), f32), pltpu.SemaphoreType.DMA((8,))],
        12, out_specs=ANY, aliases={10: 0},
    )


def solution(mesh):
    in_specs = (P("samp", "tiles"), P("tiles", "samp", None), P("tiles", None))
    out_specs = P("tiles", "samp", None)

    return jax.shard_map(shards, mesh=mesh, in_specs=in_specs, out_specs=out_specs, check_vma=False)
```

```python
import functools

import jax
import jax.numpy as jnp
from jax import lax
from jax.experimental import pallas as pl
from jax.experimental.pallas import tpu as pltpu
from jax.sharding import PartitionSpec as P


BLK_DEV = 2
step_size = 0.25
penalty = 0.2

VMEM = pl.BlockSpec(memory_space=pltpu.VMEM)
SMEM = pl.BlockSpec(memory_space=pltpu.SMEM)
ANY = pl.BlockSpec(memory_space=pl.ANY)
HBM = pl.BlockSpec(memory_space=pltpu.HBM)
bf16, f32 = jnp.bfloat16, jnp.float32

OWN_PAIR = 8
LIMIT = 12 << 20


def dot_nn(a, b):
    return jnp.dot(a, b, preferred_element_type=f32)


def dot_nt(a, b):
    return lax.dot_general(a, b, (((1,), (1,)), ((), ())), preferred_element_type=f32)


def shrink(value):
    level = step_size * penalty
    return value - jnp.clip(value, -level, level)


def shrink_diagonal(value, quarter):
    rows, width = value.shape
    row_ids = quarter * rows + lax.broadcasted_iota(jnp.int32, (rows, width), 0)
    col_ids = lax.broadcasted_iota(jnp.int32, (rows, width), 1)
    positive = 0.5 * (value + jnp.sqrt(value * value + 4.0 * step_size))
    return jnp.where(row_ids == col_ids, positive, shrink(value))


def find_slots(blocks, coords, slot_of):
    first = (lax.axis_index("tiles") - 1) * BLK_DEV
    for pair in range(OWN_PAIR + 1):
        slot_of[pair] = 0

    def place(slot, side):
        at = coords[slot, side] - first
        at = jnp.where(at < 0, at + blocks, at)
        return jnp.where(at >= blocks, at - blocks, at)

    for slot in range(BLK_DEV, coords.shape[0]):
        row, col = place(slot, 0), place(slot, 1)
        pair = jnp.where(col >= 2 * BLK_DEV, (col - 2 * BLK_DEV) * 2 * BLK_DEV + row, OWN_PAIR)
        slot_of[pair] = slot


def is_even():
    return lax.rem(lax.axis_index("tiles"), 2) == 0


def repeat_kernel(x, out, held, in_sem, out_sems):
    load = pltpu.make_async_copy(x, held, in_sem)
    load.start()
    load.wait()
    stores = [pltpu.make_async_copy(held, out.at[part], out_sems.at[part]) for part in range(out.shape[0])]
    for store in stores:
        store.start()
    for store in stores:
        store.wait()


def cut_kernel(omega, out, held, pieces, in_sems, out_sems):
    rows = omega.shape[1]
    others = held.shape[0]
    loads = [
        pltpu.make_async_copy(omega.at[BLK_DEV + k], held.at[k], in_sems.at[k]) for k in range(others)
    ]
    for load in loads:
        load.start()
    stores = []
    for k in range(others):
        loads[k].wait()
        for part in range(out.shape[0]):
            pieces[part, k] = held[k, :, part * rows : (part + 1) * rows].astype(bf16).T
        stores.append(pltpu.make_async_copy(pieces.at[:, k], out.at[:, k], out_sems.at[k]))
        stores[-1].start()
    for store in stores:
        store.wait()


def choose(even_is_first, first, second):
    even = is_even()

    @pl.when(even if even_is_first else jnp.logical_not(even))
    def _():
        first()

    @pl.when(jnp.logical_not(even) if even_is_first else even)
    def _():
        second()


def next_side():
    return jnp.where(is_even(), 2, 0)


def put_tile(slot, tile, mats, at):
    mats[at] = jnp.where(slot > 0, tile, 0.0).astype(bf16)


def spot(i, rows, start, width):
    return slice(i * rows, (i + 1) * rows), slice(start, start + width)


def first_rows(slot_of, omega, base, s_near, mats):
    rows, width = omega.shape[1:]
    for i in range(2):
        for blk in range(2):
            slot = slot_of[blk * 4 + base + i]
            put_tile(slot, omega[slot], mats, spot(i, rows, blk * width, width))
    return dot_nt(mats[...], s_near[...])


def first_cols(turned, s_near, s_own):
    rows, width = turned.shape[1:]
    total = jnp.zeros((2 * rows, s_own.shape[0]), f32)
    for a in range(2 * BLK_DEV):
        source = (s_near, s_own)[a // BLK_DEV]
        blk = a % BLK_DEV
        total += dot_nt(turned[2 * a : 2 * a + 2].reshape(2 * rows, width), source[:, blk * width : (blk + 1) * width])
    return total


def first_cross_kernel(blocks, coords, omega, parts, s_own, s_in, turned, out, s_chip, slot_of, mats, sems, s_sem):
    window = pltpu.make_async_copy(s_in, s_chip, s_sem)
    window.start()
    rows, _ = omega.shape[1:]
    count = parts.shape[0]
    find_slots(blocks, coords, slot_of)

    def fill(pair):
        slot = slot_of[pair]
        unit = OWN_PAIR if pair == OWN_PAIR else pair % 4 * 2 + pair // 4
        copies = [
            pltpu.make_async_copy(
                parts.at[part, slot - BLK_DEV],
                turned.at[unit, :, part * rows : (part + 1) * rows],
                sems.at[pair, part],
            )
            for part in range(count)
        ]
        return slot, unit, copies

    for pair in range(OWN_PAIR + 1):
        slot, unit, copies = fill(pair)

        @pl.when(slot > 0)
        def _(copies=copies):
            for copy in copies:
                copy.start()

        @pl.when(slot == 0)
        def _(unit=unit):
            turned[unit] = jnp.zeros_like(turned[unit])

    window.wait()

    @pl.when(is_even())
    def _():
        out[...] = first_rows(slot_of, omega, 0, s_chip, mats).astype(bf16)

    for pair in range(OWN_PAIR + 1):
        slot, unit, copies = fill(pair)

        @pl.when(slot > 0)
        def _(copies=copies):
            for copy in copies:
                copy.wait()

    @pl.when(jnp.logical_not(is_even()))
    def _():
        out[...] = first_cols(turned, s_chip, s_own).astype(bf16)


def first_chip_kernel(blocks, slot_of, omega, turned, s_own, s_in, out, s_cross, mats, s_sem):
    window = pltpu.make_async_copy(s_in, s_cross, s_sem)
    window.start()
    window.wait()

    def cols():
        out[...] = first_cols(turned, s_cross, s_own).astype(bf16)

    def rows():
        out[...] = first_rows(slot_of, omega, 0, s_cross, mats).astype(bf16)

    choose(True, cols, rows)


def first_own_kernel(blocks, slot_of, omega, turned, s_own, s_cross, s_chip, own, stq, mats):
    rows, width = omega.shape[1:]
    quarter = lax.axis_index("samp")
    mats[:rows, :width] = omega[0].astype(bf16)
    mats[rows:, width:] = omega[1].astype(bf16)
    slot = slot_of[OWN_PAIR]
    put_tile(slot, omega[slot], mats, spot(0, rows, width, width))
    mats[rows:, :width] = turned[OWN_PAIR]
    own[...] = dot_nt(mats[...], s_own[...])

    def add(s_next):
        own[...] += first_rows(slot_of, omega, BLK_DEV, s_next, mats)

    choose(True, lambda: add(s_chip), lambda: add(s_cross))
    for side, ref in enumerate((s_cross, s_own, s_chip)):
        for blk in range(BLK_DEV):
            at = pl.multiple_of(blk * width + quarter * rows, rows)
            stq[side, blk * rows : (blk + 1) * rows, :] = ref[:, pl.ds(at, rows)].T


def half_kernel(stq, p_own, out):
    count, both = p_own.shape[0], p_own.shape[1]
    rows = both // BLK_DEV
    far = stq[next_side()]
    for part in range(count):
        piece = dot_nt(far, p_own[part])
        for blk in range(BLK_DEV):
            at = (blk * count + part) * rows
            out[:, at : at + rows] = piece[:, blk * rows : (blk + 1) * rows]


def natural(out, pieces):
    count, both = pieces.shape[0], pieces.shape[1]
    rows = both // BLK_DEV
    for blk in range(BLK_DEV):
        for part in range(count):
            at = (blk * count + part) * rows
            out[at : at + rows, :] = pieces[part, blk * rows : (blk + 1) * rows, :]


def update_edge(old, slots, ptq, far, s_near, p_near, scale, grad, nat, put):
    rows, width = grad.shape[0] // 2, grad.shape[1] // 2
    natural(nat, p_near)
    grad[...] = dot_nn(ptq, s_near[...]) + dot_nt(far, nat[...])
    for i in range(2):
        for blk in range(2):
            slot = slots(i, blk)
            put(i, blk, slot, shrink(old(i, blk, slot) - scale * grad[spot(i, rows, blk * width, width)]))


def edge_kernel(
    blocks, far_side, slot_of, omega, turned, s_own, s_near, p_near, p_far, stq, own_half,
    tiles, out, grad, mats, nat,
):
    rows, width = omega.shape[1:]
    wide = s_own.shape[1]
    quarter = lax.axis_index("samp")
    scale = step_size / (2.0 * s_own.shape[0])

    def far_rows():
        return p_far[quarter] if far_side else p_far[...]

    def row_tiles():
        def put(i, blk, slot, tile):
            tiles[i * 2 + blk] = tile
            put_tile(slot, tile, mats, spot(i, rows, blk * width, width))

        update_edge(
            lambda i, blk, slot: omega[slot], lambda i, blk: slot_of[blk * 4 + i],
            far_rows(), stq[far_side], s_near, p_near, scale, grad, nat, put,
        )
        out[...] = dot_nt(mats[:, :wide], s_near[...]).astype(bf16)

    def col_tiles():
        def put(i, blk, slot, tile):
            put_tile(slot, tile, mats, spot(i, rows, blk * width, width))

        update_edge(
            lambda i, blk, slot: turned[2 * blk + i].astype(f32),
            lambda i, blk: slot_of[i * 4 + blk],
            far_rows(), stq[far_side], s_near, p_near, scale, grad, nat, put,
        )
        grad[...] = dot_nn(far_rows(), s_own[...]) + own_half[...]
        for i in range(2):
            for blk in range(2):
                tile = turned[2 * (BLK_DEV + blk) + i].astype(f32) - scale * grad[spot(i, rows, blk * width, width)]
                put_tile(slot_of[i * 4 + BLK_DEV + blk], shrink(tile), mats, spot(i, rows, wide + blk * width, width))
        total = dot_nt(mats[:, :wide], s_near[...]) + dot_nt(mats[:, wide:], s_own[...])
        out[...] = total.astype(bf16)

    choose(far_side == 0, row_tiles, col_tiles)


def own_kernel(blocks, slot_of, omega, turned, s_own, stq, p_own, tiles, t_own, grad, mats, nat_own):
    rows, width = grad.shape[0] // 2, grad.shape[1] // 2
    quarter = lax.axis_index("samp")
    scale = step_size / (2.0 * s_own.shape[0])
    natural(nat_own, p_own)
    grad[...] = dot_nn(p_own[quarter], s_own[...]) + dot_nt(stq[1], nat_own[...])
    slot = slot_of[OWN_PAIR]
    for i in range(BLK_DEV):
        here = grad[spot(i, rows, i * width, width)]
        tiles[i] = shrink_diagonal(omega[i] - scale * here, quarter)
        mats[spot(i, rows, i * width, width)] = tiles[i].astype(bf16)
    tiles[2] = shrink(omega[slot] - scale * grad[:rows, width:])
    put_tile(slot, tiles[2], mats, spot(0, rows, width, width))
    there = turned[OWN_PAIR].astype(f32) - scale * grad[rows:, :width]
    put_tile(slot, shrink(there), mats, spot(1, rows, 0, width))
    t_own[...] = dot_nt(mats[...], s_own[...])


def inner_kernel(
    blocks, slot_of, omega, s_cross, s_chip, stq, p_own, p_cross, p_chip, t_own, tiles, own, grad, mats, nat
):
    rows, width = omega.shape[1:]
    quarter = lax.axis_index("samp")
    scale = step_size / (2.0 * s_chip.shape[0])

    def put(i, blk, slot, tile):
        tiles[i * 2 + blk] = tile
        put_tile(slot, tile, mats, spot(i, rows, blk * width, width))

    def run(s_next, p_next):
        update_edge(
            lambda i, blk, slot: omega[slot],
            lambda i, blk: slot_of[blk * 4 + BLK_DEV + i],
            p_own[quarter], stq[1], s_next, p_next, scale, grad, nat, put,
        )
        own[...] = t_own[...] + dot_nt(mats[...], s_next[...])

    choose(True, lambda: run(s_chip, p_chip), lambda: run(s_cross, p_cross))


def own_last_kernel(
    blocks, slot_of, held, s_own, s_cross, s_chip, stq, p_own, out, rows_half, grad, nat_own, tiles, sems,
):
    rows, width = grad.shape[0] // 2, grad.shape[1] // 2
    quarter = lax.axis_index("samp")
    scale = step_size / (2.0 * s_own.shape[0])
    natural(nat_own, p_own)
    grad[...] = dot_nn(p_own[quarter], s_own[...]) + dot_nt(stq[1], nat_own[...])
    slot = slot_of[OWN_PAIR]
    copies = [pltpu.make_async_copy(tiles.at[i], out.at[i], sems.at[i]) for i in range(BLK_DEV)]
    copies.append(pltpu.make_async_copy(tiles.at[2], out.at[slot], sems.at[2]))
    for i in range(BLK_DEV):
        here = grad[i * rows : (i + 1) * rows, i * width : (i + 1) * width]
        tiles[i] = shrink_diagonal(held[i] - scale * here, quarter)
        copies[i].start()
    tiles[2] = shrink(held[2] - scale * grad[:rows, width:])

    @pl.when(slot > 0)
    def _():
        copies[2].start()

    def half(s_next):
        rows_half[...] = dot_nn(p_own[quarter], s_next[...])

    choose(True, lambda: half(s_chip), lambda: half(s_cross))
    for i in range(BLK_DEV):
        copies[i].wait()

    @pl.when(slot > 0)
    def _():
        copies[2].wait()


def last_kernel(
    blocks, slot_of, outer_cross, outer_chip, inner, s_cross, s_chip, stq, rows_half, p_cross, p_chip, begun,
    out, grad, nat, tiles, sems,
):
    rows, width = tiles.shape[1:]
    quarter = lax.axis_index("samp")
    scale = step_size / (2.0 * s_chip.shape[0])

    def copy(unit, slot):
        return pltpu.make_async_copy(tiles.at[unit], out.at[slot], sems.at[unit])

    def slot_at(group, i, blk):
        return slot_of[blk * 4 + group * BLK_DEV + i]

    def run(outer, s_next, p_next, p_far, far):
        natural(nat, p_next)
        for group in (1, 0):
            other = rows_half[...] if group else dot_nn(p_far[quarter], s_next[...])
            grad[group] = other + dot_nt((far, stq[1])[group], nat[...])
            for i in range(2):
                for blk in range(2):
                    here = grad[(group,) + spot(i, rows, blk * width, width)]
                    unit, slot = group * 4 + i * 2 + blk, slot_at(group, i, blk)
                    tiles[unit] = shrink((outer, inner)[group][i * 2 + blk] - scale * here)

                    @pl.when(slot > 0)
                    def _(unit=unit, slot=slot):
                        copy(unit, slot).start()

    choose(
        True,
        lambda: run(outer_cross, s_chip, p_chip, p_cross, stq[0]),
        lambda: run(outer_chip, s_cross, p_cross, p_chip, stq[2]),
    )
    for group in range(2):
        for i in range(2):
            for blk in range(2):
                unit, slot = group * 4 + i * 2 + blk, slot_at(group, i, blk)

                @pl.when(slot > 0)
                def _(unit=unit, slot=slot):
                    copy(unit, slot).wait()


def shards(samples, omega, coords):
    size = lax.axis_size("tiles")
    parts = lax.axis_size("samp")
    blocks = BLK_DEV * size
    tiles, rows, width = omega.shape
    others = tiles - BLK_DEV
    count = samples.shape[0] * parts
    wide = samples.shape[1]
    both = BLK_DEV * rows
    chip = [(i, i ^ 1) for i in range(size)]
    cross = [(i, (i - 1) % size if i % 2 == 0 else (i + 1) % size) for i in range(size)]
    shape = jax.ShapeDtypeStruct
    params = pltpu.CompilerParams(vmem_limit_bytes=LIMIT)

    def call(body, in_specs, outs, scratch, macs, moved, aliases=None, out_specs=None):
        several = isinstance(outs, tuple)
        specs = out_specs or ((VMEM,) * len(outs) if several else VMEM)
        return pl.pallas_call(
            body, out_shape=outs, in_specs=in_specs, out_specs=specs, scratch_shapes=scratch,
            compiler_params=params, input_output_aliases=aliases or {},
            cost_estimate=pl.CostEstimate(flops=2 * macs, bytes_accessed=moved, transcendentals=0),
        )

    def permute(x, pairs):
        return lax.ppermute(x, "tiles", pairs)

    def spread(x):
        return lax.all_to_all(jnp.broadcast_to(x[None], (parts,) + x.shape), "samp", 0, 0)

    copies = call(
        repeat_kernel, [HBM], pltpu.HBM((parts,) + samples.shape, bf16),
        [pltpu.VMEM(samples.shape, bf16), pltpu.SemaphoreType.DMA, pltpu.SemaphoreType.DMA((parts,))],
        0, 1 << 20, out_specs=HBM,
    )(pltpu.with_memory_space_constraint(samples, pltpu.HBM))
    s_own = lax.all_to_all(copies, "samp", 0, 0).reshape(count, wide)
    pieces = call(
        cut_kernel, [HBM], pltpu.HBM((parts, others, rows, rows), bf16),
        [
            pltpu.VMEM((others, rows, width), f32), pltpu.VMEM((parts, others, rows, rows), bf16),
            pltpu.SemaphoreType.DMA((others,)), pltpu.SemaphoreType.DMA((others,)),
        ],
        0, 4 << 20, out_specs=HBM,
    )(pltpu.with_memory_space_constraint(omega, pltpu.HBM))
    turned_parts = lax.all_to_all(pieces, "samp", 0, 0)
    s_cross = permute(s_own, cross)
    s_chip = permute(s_own, chip)

    part = shape((both, count), bf16)
    full = shape((both, count), f32)
    four = shape((4, rows, width), f32)
    wide_half = shape((both, wide), f32)
    unit = rows * width * count
    grad = pltpu.VMEM((both, wide), f32)
    mats = pltpu.VMEM((both, wide), bf16)
    mats_two = pltpu.VMEM((both, 2 * wide), bf16)
    nat = pltpu.VMEM((wide, count), bf16)

    def run(body, args, in_specs, outs, scratch, units, out_specs=None, aliases=None):
        return call(body, in_specs, outs, scratch, units * unit, 4 << 20, aliases, out_specs)(*args)

    def kernel(body, *extra):
        return functools.partial(body, blocks, *extra)

    turned, to_cross, s_chip, slot_of = run(
        kernel(first_cross_kernel), (coords, omega, turned_parts, s_own, s_chip), [SMEM, VMEM, ANY, VMEM, ANY],
        (
            shape((OWN_PAIR + 1, rows, width), bf16), part, shape((count, wide), bf16),
            shape((OWN_PAIR + 1,), jnp.int32),
        ),
        [mats, pltpu.SemaphoreType.DMA((OWN_PAIR + 1, parts)), pltpu.SemaphoreType.DMA], 8,
        out_specs=(VMEM, VMEM, VMEM, SMEM),
    )
    from_cross = permute(to_cross, cross)
    to_chip, s_cross = run(
        kernel(first_chip_kernel), (slot_of, omega, turned, s_own, s_cross), [SMEM] + [VMEM] * 3 + [ANY],
        (part, shape((count, wide), bf16)), [mats, pltpu.SemaphoreType.DMA], 8,
    )
    from_chip = permute(to_chip, chip)
    own, stq = run(
        kernel(first_own_kernel), (slot_of, omega, turned, s_own, s_cross, s_chip), [SMEM] + [VMEM] * 5,
        (full, shape((3, both, count), bf16)), [mats], 8,
    )
    total = (own + from_cross.astype(f32) + from_chip.astype(f32)).astype(bf16)
    far_cross = permute(total, cross)
    p_own = spread(total)
    p_cross = permute(p_own, cross)
    p_chip = permute(p_own, chip)
    own_half = run(half_kernel, (stq, p_own), [VMEM] * 2, wide_half, [], 4)

    def edge(side, s_near, p_near, p_far):
        return run(
            kernel(edge_kernel, side), (slot_of, omega, turned, s_own, s_near, p_near, p_far, stq, own_half),
            [SMEM] + [VMEM] * 8, (four, part), [grad, mats_two, nat], 20,
        )

    outer_cross, to_cross = edge(0, s_chip, p_chip, far_cross)
    from_cross = permute(to_cross, cross)
    mine, t_own = run(
        kernel(own_kernel), (slot_of, omega, turned, s_own, stq, p_own), [SMEM] + [VMEM] * 5,
        (shape((3, rows, width), f32), full), [grad, mats, nat], 12,
    )
    outer_chip, to_chip = edge(2, s_cross, p_cross, p_chip)
    from_chip = permute(to_chip, chip)
    inner, own = run(
        kernel(inner_kernel), (slot_of, omega, s_cross, s_chip, stq, p_own, p_cross, p_chip, t_own),
        [SMEM] + [VMEM] * 8, (four, full), [grad, mats, nat], 12,
    )
    total = (own + from_cross.astype(f32) + from_chip.astype(f32)).astype(bf16)
    p_own = spread(total)
    p_cross = permute(p_own, cross)
    p_chip = permute(p_own, chip)
    whole = shape(omega.shape, f32)
    begun, rows_half = run(
        kernel(own_last_kernel), (slot_of, mine, s_own, s_cross, s_chip, stq, p_own), [SMEM] + [VMEM] * 6,
        (whole, wide_half),
        [grad, nat, pltpu.VMEM((3, rows, width), f32), pltpu.SemaphoreType.DMA((3,))],
        12, out_specs=(ANY, VMEM),
    )
    return run(
        kernel(last_kernel),
        (slot_of, outer_cross, outer_chip, inner, s_cross, s_chip, stq, rows_half, p_cross, p_chip, begun),
        [SMEM] + [VMEM] * 9 + [ANY], whole,
        [pltpu.VMEM((2, both, wide), f32), nat, pltpu.VMEM((8, rows, width), f32), pltpu.SemaphoreType.DMA((8,))],
        12, out_specs=ANY, aliases={10: 0},
    )


def solution(mesh):
    in_specs = (P("samp", "tiles"), P("tiles", "samp", None), P("tiles", None))
    out_specs = P("tiles", "samp", None)

    return jax.shard_map(shards, mesh=mesh, in_specs=in_specs, out_specs=out_specs, check_vma=False)
```
